256 devices in a mesh: blk: 32 (over x, y, z_lo), seg: 8 (over z_hi, core).
Axes of the slice: x: 4, y: 4, z: 8 (z_hi: 4, z_lo: 2; z = z_hi * 2 + z_lo), core: 2. Of those that a mesh axis runs over, the one named last changes fastest.
Arguments:
- spectra: bfloat16 [112, 2048, 2, 512], P('seg', 'blk'), as said below
- valid_flags: int32 [112, 2048], P('seg', 'blk'), may hold values 0 or 1
Outputs:
- correlations: bfloat16 [2, 2048, 64, 1024], P(None, ('blk', 'seg'))
The draws below stay inside these ranges and needn't reach their ends.
Inputs may be any that keep to these rules, and one draw needn't show every extreme that they name: `spectra`: rough spectral values; their scale varies from bin to bin, channel to channel and window to window.
All inputs are finite; a program needn't handle non-finite values. No bound on the sum of `valid_flags` on one device may be relied on, other than what follows from the above.
Results may differ from the reference program's by a relative error of at most 0.015.
Values may be sent and summed in bfloat16 or wider, within the bound.
No kernel may reach another device: no remote copies, remote signals or barrier semaphores. Data moves between devices by JAX's collectives and lax.ppermute only.
A program may use at most 128 MiB of HBM per device.

```python
import math
import jax
import jax.numpy as jnp
from jax import lax

CHANNELS = 2048
FREQ_BINS = 512
LAG_COUNT = 1024
WIN_SAMPLES = 15000
BAND_START = 30
SMOOTH_HALF = 32
ROUNDS = 2
WIN_DEV = 14
WINDOWS = 112
N_BLK = 32
N_SEG = 8


def draw_spectra(key, part):
    key_base, key_bins, key_traces = jax.random.split(key, 3)
    full_shape = (WINDOWS, CHANNELS, 2, FREQ_BINS)
    base_draw = jax.random.truncated_normal(key_base, -5.0, 5.0, full_shape, jnp.float32)
    trace_span = math.log(10.0)
    bin_scale = jnp.exp(jax.random.uniform(key_bins, (1, CHANNELS, 1, FREQ_BINS), jnp.float32, 0.0, math.log(10.0)))
    trace_scale = jnp.exp(jax.random.uniform(key_traces, (WINDOWS, CHANNELS, 1, 1), jnp.float32, 0.0, trace_span))
    return (base_draw * bin_scale * trace_scale).astype(jnp.bfloat16)


def touch_ends(array, key, smallest, top_value):
    longest = array.shape.index(max(array.shape))
    spots = []
    for shift in (0, 1):
        where = [jax.random.randint(jax.random.fold_in(key, axis), (), 0, length) for axis, length in enumerate(array.shape)]
        where[longest] = (where[longest] + shift) % array.shape[longest]
        spots.append(tuple(where))
    return array.at[spots[0]].set(smallest).at[spots[1]].set(top_value)


def setup_inputs(seed: int = 0) -> dict:
    streams_of = jax.random.split(jax.random.key(seed), 3)
    return {
        "spectra": draw_spectra(jax.random.fold_in(streams_of[2], 71), 0),
        "valid_flags": touch_ends((jax.random.randint(streams_of[1], (WINDOWS, CHANNELS), 0, 8) < 7).astype(jnp.int32), jax.random.fold_in(streams_of[1], 1), 0, 1),
    }


def lag_table(bin_count, lag_count):
    freq_ids = lax.broadcasted_iota(jnp.int32, (bin_count, lag_count), 0) + BAND_START
    delay_ids = lax.broadcasted_iota(jnp.int32, (bin_count, lag_count), 1) - lag_count // 2
    angles = jnp.mod(freq_ids * delay_ids, WIN_SAMPLES).astype(jnp.float32) * (2.0 * math.pi / WIN_SAMPLES)
    return jnp.stack([jnp.cos(angles), -jnp.sin(angles)], axis=1).astype(jnp.bfloat16)

def smooth_sum(values):
    bin_count = values.shape[-1]
    widths = [(0, 0)] * (values.ndim - 1) + [(SMOOTH_HALF, SMOOTH_HALF)]
    padded = jnp.pad(values, widths)
    total = jnp.zeros_like(values)
    for offset in range(2 * SMOOTH_HALF + 1):
        total = total + padded[..., offset:offset + bin_count]
    return total

def whiten_block(spectra_block, flags_block):
    real_part = spectra_block[:, :, 0, :].astype(jnp.float32)
    imag_part = spectra_block[:, :, 1, :].astype(jnp.float32)
    amplitude = jnp.sqrt(real_part * real_part + imag_part * imag_part).astype(jnp.bfloat16)
    amplitude_wide = lax.optimization_barrier(amplitude).astype(jnp.float32)
    counts = smooth_sum(jnp.ones((FREQ_BINS,), jnp.float32))
    smooth = smooth_sum(amplitude_wide) / counts
    scaling = flags_block.astype(jnp.float32)[:, :, None] / (smooth + 1e-05)
    return (spectra_block.astype(jnp.float32) * scaling[:, :, None, :]).astype(jnp.bfloat16)

def reference(spectra, valid_flags):
    block_width = CHANNELS // N_BLK
    block_ids = jnp.arange(N_BLK, dtype=jnp.int32)

    def whiten_one(block_id):
        start = (block_id * block_width).astype(jnp.int32)
        piece = lax.dynamic_slice_in_dim(spectra, start, block_width, 1)
        flags_piece = lax.dynamic_slice_in_dim(valid_flags, start, block_width, 1)
        return whiten_block(piece, flags_piece)
    whitened_all = lax.map(whiten_one, block_ids)
    table = lax.optimization_barrier(lag_table(FREQ_BINS, LAG_COUNT)).astype(jnp.float32)
    scaling = 1.0 / math.sqrt(WINDOWS * FREQ_BINS)
    outputs = []
    for rounds_done in range(ROUNDS):

        def one_block(block_id):
            partner_id = jnp.mod(block_id - rounds_done - 1, N_BLK).astype(jnp.int32)
            owned = whitened_all[block_id].astype(jnp.float32).reshape(N_SEG, WIN_DEV, block_width, 2, FREQ_BINS)
            partner = whitened_all[partner_id].astype(jnp.float32).reshape(N_SEG, WIN_DEV, block_width, 2, FREQ_BINS)
            rotated = jnp.stack([-partner[:, :, :, 1, :], partner[:, :, :, 0, :]], axis=3)
            stacked = jnp.stack([partner, rotated], axis=0)
            partials = jnp.einsum('swicf,kswjcf->sfikj', owned, stacked)
            rounded = lax.optimization_barrier(partials.astype(jnp.bfloat16)).astype(jnp.float32)
            stack = lax.optimization_barrier(jnp.sum(rounded, axis=0)).astype(jnp.bfloat16)
            stack_wide = lax.optimization_barrier(stack).astype(jnp.float32)
            result = jnp.einsum('fikj,fkl->ijl', stack_wide, table) * scaling
            return result.astype(jnp.bfloat16)
        per_block = lax.map(one_block, block_ids)
        outputs.append(per_block.reshape(CHANNELS, block_width, LAG_COUNT))
    return jnp.stack(outputs)
```

```python
import functools
import math

import jax
import jax.numpy as jnp
from jax import lax
from jax.experimental import pallas as pl
from jax.experimental.pallas import tpu as pltpu
from jax.sharding import Mesh, PartitionSpec as P

LAG_COUNT = 1024
WIN_SAMPLES = 15000
BAND_START = 30
SMOOTH_HALF = 32
BINS = 512
WIN = 14
CH = 64
CHUNKS = 2
FC = 32 // CHUNKS
CBINS = BINS // CHUNKS
F32 = jnp.float32
BF16 = jnp.bfloat16

VM = pl.BlockSpec(memory_space=pltpu.VMEM)
SM = pl.BlockSpec(memory_space=pltpu.SMEM)


def params():
    return pltpu.CompilerParams(vmem_limit_bytes=48 << 20)


def whiten_kernel(pos_ref, spec_ref, flags_ref, *refs):
    outs = refs[: 8 * CHUNKS]
    band, eye, invc, white = refs[8 * CHUNKS :]
    w = pl.program_id(0)
    z, c = pos_ref[0], pos_ref[1]

    @pl.when(w == 0)
    def _():
        rows = lax.broadcasted_iota(jnp.int32, (BINS, BINS), 0)
        cols = lax.broadcasted_iota(jnp.int32, (BINS, BINS), 1)
        band[...] = jnp.where(jnp.abs(rows - cols) <= SMOOTH_HALF, 1.0, 0.0).astype(BF16)
        r2 = lax.broadcasted_iota(jnp.int32, (256, 256), 0)
        c2 = lax.broadcasted_iota(jnp.int32, (256, 256), 1)
        eye[...] = jnp.where(r2 == c2, 1.0, 0.0).astype(BF16)
        f = lax.broadcasted_iota(jnp.int32, (BINS, 128), 0)
        count = jnp.minimum(f + SMOOTH_HALF, BINS - 1) - jnp.maximum(f - SMOOTH_HALF, 0) + 1
        invc[...] = 1.0 / count.astype(F32)

    re16, im16 = spec_ref[0, 0], spec_ref[1, 0]
    re, im = re16.astype(F32), im16.astype(F32)
    amp = jnp.sqrt(re * re + im * im).astype(BF16)
    amp2 = jnp.concatenate([amp, amp], axis=0)
    both = jnp.concatenate([re16, im16], axis=0)
    nt = (((1,), (1,)), ((), ()))
    summed = lax.dot_general(band[...], amp2, nt, preferred_element_type=F32)
    scale = flags_ref[0] / (summed * invc[...] + 1e-05)
    for h in range(2):
        half = lax.dot_general(
            eye[...], both[:, h * 256 : (h + 1) * 256], nt, preferred_element_type=F32
        )
        white[h * 256 : (h + 1) * 256] = half * scale[h * 256 : (h + 1) * 256]
    for k in range(CHUNKS):
        for r in range(8):
            base = k * CBINS + ((z + r) & 7) * (2 * FC)
            for crel in range(2):
                start = pl.multiple_of(base + (c ^ crel) * FC, FC)
                outs[k * 8 + r][crel, w] = white[pl.ds(start, FC), :].astype(BF16)


def whiten(spec, flags2, pos):
    shape = jax.ShapeDtypeStruct((2, WIN, FC, 128), BF16)
    full = pl.BlockSpec((2, WIN, FC, 128), lambda w, *_: (0, 0, 0, 0))
    return pl.pallas_call(
        whiten_kernel,
        out_shape=[shape] * (8 * CHUNKS),
        grid_spec=pltpu.PrefetchScalarGridSpec(
            num_scalar_prefetch=1,
            grid=(WIN,),
            in_specs=[
                pl.BlockSpec((2, 1, CH, BINS), lambda w, *_: (0, w, 0, 0)),
                pl.BlockSpec((1, 1, 128), lambda w, *_: (w, 0, 0)),
            ],
            out_specs=[full] * (8 * CHUNKS),
            scratch_shapes=[
                pltpu.VMEM((BINS, BINS), BF16),
                pltpu.VMEM((256, 256), BF16),
                pltpu.VMEM((BINS, 128), F32),
                pltpu.VMEM((BINS, 128), F32),
            ],
        ),
        compiler_params=params(),
        cost_estimate=pl.CostEstimate(
            flops=3 * 512 * 512 * 128 * WIN, bytes_accessed=4 << 20, transcendentals=0
        ),
        name="whiten",
    )(pos, spec, flags2)


def merge_kernel(pos_ref, *refs):
    ins, (same, other) = refs[:8], refs[8:]
    z = pos_ref[0]
    for r in range(8):
        src = (z - r) & 7
        same[src & 1, src >> 1] = ins[r][0]
        other[src & 1, src >> 1] = ins[r][1]


def merge(pieces, pos):
    shape = jax.ShapeDtypeStruct((2, 4, WIN, FC, 128), BF16)
    return pl.pallas_call(
        merge_kernel,
        out_shape=[shape] * 2,
        in_specs=[SM] + [VM] * 8,
        out_specs=[VM] * 2,
        compiler_params=params(),
        cost_estimate=pl.CostEstimate(
            flops=0, bytes_accessed=4 * 8 * WIN * FC * 256, transcendentals=0
        ),
        name="merge",
    )(pos, *pieces)


def cross_kernel(pos_ref, own0, own1, prev0, prev1, *refs):
    outs, (wide, res) = refs[:8], refs[8:]
    z, c = pos_ref[0], pos_ref[1]
    rows = 4 * WIN * FC
    for n, (first, second) in enumerate(((own0, own1), (prev0, prev1))):
        for b in range(2):
            base = (n * 2 + b) * 2 * rows
            wide[base : base + rows] = first[b].reshape(rows, 128).astype(F32)
            wide[base + rows : base + 2 * rows] = second[b].reshape(rows, 128).astype(F32)
    sign = jnp.where(lax.broadcasted_iota(jnp.int32, (CH, 128), 1) < CH, 1.0, -1.0).astype(F32)
    tn = (((0,), (0,)), ((), ()))

    def one_bin(f, carry):
        x = [
            wide[pl.ds(n * 2 * rows + f, 8 * WIN, stride=FC), :].astype(BF16) for n in range(4)
        ]
        own_a, own_b, prev_a, prev_b = x
        for b, (left, rights) in enumerate(
            ((own_a, (prev_b, prev_a)), (own_b, (own_a, prev_b)))
        ):
            g = lax.dot_general(
                left, jnp.concatenate(rights, axis=1), tn, preferred_element_type=F32
            )
            for rnd in range(2):
                top = g[:CH, rnd * 128 : rnd * 128 + 128]
                bottom = pltpu.roll(g[CH:, rnd * 128 : rnd * 128 + 128], CH, 1)
                start = pl.multiple_of(((rnd * 2 + b) * FC + f) * CH, CH)
                res[pl.ds(start, CH), :] = bottom + sign * top
        return carry

    lax.fori_loop(0, FC, one_bin, 0, unroll=2)
    for r in range(8):
        dst = (z + r) & 7
        for crel in range(2):
            row = ((dst >> 1) * 2 + (c ^ crel)) * 8
            for rnd in range(2):
                base = (rnd * 2 + (dst & 1)) * FC * CH + row
                for i in range(8):
                    outs[r][crel, rnd, i] = res[pl.ds(base + i, FC, stride=CH), :].astype(BF16)


def cross(own0, own1, prev0, prev1, pos):
    shape = jax.ShapeDtypeStruct((2, 2, 8, FC, 128), BF16)
    return pl.pallas_call(
        cross_kernel,
        out_shape=[shape] * 8,
        in_specs=[SM] + [VM] * 4,
        out_specs=[VM] * 8,
        scratch_shapes=[
            pltpu.VMEM((32 * WIN * FC, 128), F32),
            pltpu.VMEM((4 * FC * CH, 128), F32),
        ],
        compiler_params=params(),
        cost_estimate=pl.CostEstimate(
            flops=4 * FC * 128 * 256 * 256, bytes_accessed=3 << 20, transcendentals=0
        ),
        name="cross",
    )(pos, own0, own1, prev0, prev1)


def turn_kernel(pos_ref, *refs):
    ins, (same, other, buf) = refs[:8], refs[8:]
    z = pos_ref[0]
    for crel, out in enumerate((same, other)):
        for rnd in range(2):
            for i in range(8):
                for r in range(8):
                    start = pl.multiple_of(((z - r) & 7) * FC, FC)
                    buf[pl.ds(start, FC), :] = ins[r][crel, rnd, i].astype(F32)
                out[rnd, i] = buf[...].T.astype(BF16)


def turn(pieces, pos):
    shape = jax.ShapeDtypeStruct((2, 8, 128, 8 * FC), BF16)
    return pl.pallas_call(
        turn_kernel,
        out_shape=[shape] * 2,
        in_specs=[SM] + [VM] * 8,
        out_specs=[VM] * 2,
        scratch_shapes=[pltpu.VMEM((8 * FC, 128), F32)],
        compiler_params=params(),
        cost_estimate=pl.CostEstimate(flops=0, bytes_accessed=4 << 20, transcendentals=0),
        name="turn",
    )(pos, *pieces)


def invert_kernel(scaling, *refs):
    parts, (table, out) = refs[: 2 * CHUNKS], refs[2 * CHUNKS :]
    rows = []
    for i in range(4):
        cols = [p[0, i, k * CH : (k + 1) * CH] for k in range(2) for p in parts]
        rows.append(jnp.concatenate(cols, axis=1))
    left = jnp.concatenate(rows, axis=0)
    result = jnp.dot(left, table[...], preferred_element_type=F32) * scaling
    out[0] = result.reshape(4, CH, LAG_COUNT).astype(BF16)


def invert(parts, table, scaling):
    part = pl.BlockSpec((1, 4, 128, 8 * FC), lambda r, i: (r, i, 0, 0))
    return pl.pallas_call(
        functools.partial(invert_kernel, scaling),
        out_shape=jax.ShapeDtypeStruct((2, 8, CH, LAG_COUNT), BF16),
        grid=(2, 2),
        in_specs=[part] * (2 * CHUNKS) + [pl.BlockSpec((2 * BINS, LAG_COUNT), lambda r, i: (0, 0))],
        out_specs=pl.BlockSpec((1, 4, CH, LAG_COUNT), lambda r, i: (r, i, 0, 0)),
        compiler_params=params(),
        cost_estimate=pl.CostEstimate(
            flops=2 * 1024 * 1024 * 1024, bytes_accessed=6 << 20, transcendentals=0
        ),
        name="invert",
    )(*parts, table)


def lag_table(core):
    n = lax.broadcasted_iota(jnp.int32, (BINS, LAG_COUNT), 0)
    fine = n % FC
    z = (n // FC) % 8
    part = (n // (8 * FC)) % 2
    chunk = n // (16 * FC)
    freq_ids = chunk * CBINS + z * (2 * FC) + (part ^ core) * FC + fine + BAND_START
    delay_ids = lax.broadcasted_iota(jnp.int32, (BINS, LAG_COUNT), 1) - LAG_COUNT // 2
    angles = jnp.mod(freq_ids * delay_ids, WIN_SAMPLES).astype(F32) * (2.0 * math.pi / WIN_SAMPLES)
    return jnp.concatenate([jnp.cos(angles), -jnp.sin(angles)], axis=0).astype(BF16)


def place(z):
    return (z % 2) * 4 + z // 2


def ring(value, shift):
    return lax.ppermute(
        value, ("zl", "zh"), [(place(z), place((z + shift) % 8)) for z in range(8)]
    )


def other_core(value):
    return lax.ppermute(value, "c", [(0, 1), (1, 0)])


def shards(spectra, valid_flags):
    z = 2 * lax.axis_index("zh") + lax.axis_index("zl")
    c = lax.axis_index("c")
    pos = jnp.stack([z, c]).astype(jnp.int32)
    windows = spectra.shape[0] * lax.axis_size(("zh", "c"))
    scaling = 1.0 / math.sqrt(windows * BINS)
    flags = valid_flags.astype(F32)
    flags2 = jnp.concatenate([flags, flags], axis=1)[:, None, :]
    white = whiten(jnp.transpose(spectra, (2, 0, 1, 3)), flags2, pos)
    table = lag_table(c)
    up = [(i, (i + 1) % 16) for i in range(16)]
    swap = [(2 * i + k, 2 * j + 1 - k) for i, j in up for k in range(2)]
    parts = []
    for k in range(CHUNKS):
        out = white[k * 8 : k * 8 + 8]
        got = [out[0]] + [ring(out[r], r) for r in range(1, 8)]
        same, other = merge(got, pos)
        prev0 = lax.ppermute(same, ("x", "y"), up)
        prev1 = lax.ppermute(other, ("x", "y", "c"), swap)
        own1 = other_core(other)
        out = cross(same, own1, prev0, prev1, pos)
        got = [out[0]] + [ring(out[r], r) for r in range(1, 8)]
        same, other = turn(got, pos)
        parts += [same, other_core(other)]
    return invert(parts, table, scaling)


def solution(mesh):
    grid = mesh.devices.reshape(4, 4, 2, 4, 2)
    fine = Mesh(grid, ("x", "y", "zl", "zh", "c"))
    blk, seg = ("x", "y", "zl"), ("zh", "c")
    in_specs = (P(seg, blk, None, None), P(seg, blk))
    out_specs = P(None, blk + seg, None, None)
    return jax.shard_map(shards, mesh=fine, in_specs=in_specs, out_specs=out_specs, check_vma=False)
```

```python
import functools
import math

import jax
import jax.numpy as jnp
from jax import lax
from jax.experimental import pallas as pl
from jax.experimental.pallas import tpu as pltpu
from jax.sharding import Mesh, PartitionSpec as P


LAG_COUNT = 1024
WIN_SAMPLES = 15000
BAND_START = 30
SMOOTH_HALF = 32
BINS = 512
WIN = 14
CH = 64
CHUNKS = 2
FC = 32 // CHUNKS
CBINS = BINS // CHUNKS
F32 = jnp.float32
BF16 = jnp.bfloat16

VM = pl.BlockSpec(memory_space=pltpu.VMEM)
SM = pl.BlockSpec(memory_space=pltpu.SMEM)
ANY = pl.BlockSpec(memory_space=pl.ANY)


def params():
    return pltpu.CompilerParams(vmem_limit_bytes=48 << 20)


def whiten_kernel(pos_ref, spec_ref, flags_ref, *refs):
    outs = refs[: 8 * CHUNKS]
    band, eye, invc, white = refs[8 * CHUNKS :]
    w = pl.program_id(0)
    z, c = pos_ref[0], pos_ref[1]

    @pl.when(w == 0)
    def _():
        rows = lax.broadcasted_iota(jnp.int32, (BINS, BINS), 0)
        cols = lax.broadcasted_iota(jnp.int32, (BINS, BINS), 1)
        band[...] = jnp.where(jnp.abs(rows - cols) <= SMOOTH_HALF, 1.0, 0.0).astype(BF16)
        r2 = lax.broadcasted_iota(jnp.int32, (256, 256), 0)
        c2 = lax.broadcasted_iota(jnp.int32, (256, 256), 1)
        eye[...] = jnp.where(r2 == c2, 1.0, 0.0).astype(BF16)
        f = lax.broadcasted_iota(jnp.int32, (BINS, 128), 0)
        count = jnp.minimum(f + SMOOTH_HALF, BINS - 1) - jnp.maximum(f - SMOOTH_HALF, 0) + 1
        invc[...] = 1.0 / count.astype(F32)

    re16, im16 = spec_ref[0, 0], spec_ref[1, 0]
    re, im = re16.astype(F32), im16.astype(F32)
    amp = jnp.sqrt(re * re + im * im).astype(BF16)
    amp2 = jnp.concatenate([amp, amp], axis=0)
    both = jnp.concatenate([re16, im16], axis=0)
    nt = (((1,), (1,)), ((), ()))
    summed = lax.dot_general(band[...], amp2, nt, preferred_element_type=F32)
    scale = flags_ref[0] / (summed * invc[...] + 1e-05)
    for h in range(2):
        half = lax.dot_general(
            eye[...], both[:, h * 256 : (h + 1) * 256], nt, preferred_element_type=F32
        )
        white[h * 256 : (h + 1) * 256] = (half * scale[h * 256 : (h + 1) * 256]).astype(BF16)
    for k in range(CHUNKS):
        for r in range(8):
            base = k * CBINS + ((z + r) & 7) * (2 * FC)
            for crel in range(2):
                start = pl.multiple_of(base + (c ^ crel) * FC, FC)
                outs[k * 8 + r][crel, w] = white[pl.ds(start, FC), :]


def whiten(spec, flags2, pos):
    shape = jax.ShapeDtypeStruct((2, WIN, FC, 128), BF16)
    full = pl.BlockSpec((2, WIN, FC, 128), lambda w, *_: (0, 0, 0, 0))
    return pl.pallas_call(
        whiten_kernel,
        out_shape=[shape] * (8 * CHUNKS),
        grid_spec=pltpu.PrefetchScalarGridSpec(
            num_scalar_prefetch=1,
            grid=(WIN,),
            in_specs=[
                pl.BlockSpec((2, 1, CH, BINS), lambda w, *_: (0, w, 0, 0)),
                pl.BlockSpec((1, 1, 128), lambda w, *_: (w, 0, 0)),
            ],
            out_specs=[full] * (8 * CHUNKS),
            scratch_shapes=[
                pltpu.VMEM((BINS, BINS), BF16),
                pltpu.VMEM((256, 256), BF16),
                pltpu.VMEM((BINS, 128), F32),
                pltpu.VMEM((BINS, 128), BF16),
            ],
        ),
        compiler_params=params(),
        cost_estimate=pl.CostEstimate(
            flops=3 * 512 * 512 * 128 * WIN, bytes_accessed=4 << 20, transcendentals=0
        ),
        name="whiten",
    )(pos, spec, flags2)


def merge_kernel(pos_ref, *refs):
    ins, (same, other, core) = refs[:8], refs[-3:]
    z = pos_ref[0]
    core[0] = pos_ref[1]
    for r in range(8):
        src = (z - r) & 7
        same[src & 1, src >> 1] = ins[r][0]
        other[src & 1, src >> 1] = ins[r][1]


def merge(pieces, pos, *after):
    shape = jax.ShapeDtypeStruct((2, 4, WIN, FC, 128), BF16)
    return pl.pallas_call(
        merge_kernel,
        out_shape=[shape] * 2 + [jax.ShapeDtypeStruct((1,), jnp.int32)],
        in_specs=[SM] + [VM] * 8 + [ANY] * len(after),
        out_specs=[VM] * 2 + [SM],
        compiler_params=params(),
        cost_estimate=pl.CostEstimate(
            flops=0, bytes_accessed=4 * 8 * WIN * FC * 256, transcendentals=0
        ),
        name="merge",
    )(pos, *pieces, *after)


def cross_kernel(pos_ref, own0, own1, prev0, prev1, *refs):
    outs, (wide, res) = refs[-10:-2], refs[-2:]
    z, c = pos_ref[0], pos_ref[1]
    rows = 4 * WIN * FC
    for n, (first, second) in enumerate(((own0, own1), (prev0, prev1))):
        for b in range(2):
            base = (n * 2 + b) * 2 * rows
            wide[base : base + rows] = first[b].reshape(rows, 128).astype(F32)
            wide[base + rows : base + 2 * rows] = second[b].reshape(rows, 128).astype(F32)
    sign = jnp.where(lax.broadcasted_iota(jnp.int32, (CH, 128), 1) < CH, 1.0, -1.0).astype(F32)
    tn = (((0,), (0,)), ((), ()))

    def one_bin(f, carry):
        x = [
            wide[pl.ds(n * 2 * rows + f, 8 * WIN, stride=FC), :].astype(BF16) for n in range(4)
        ]
        own_a, own_b, prev_a, prev_b = x
        for b, (left, rights) in enumerate(
            ((own_a, (prev_b, prev_a)), (own_b, (own_a, prev_b)))
        ):
            g = lax.dot_general(
                left, jnp.concatenate(rights, axis=1), tn, preferred_element_type=F32
            )
            for rnd in range(2):
                top = g[:CH, rnd * 128 : rnd * 128 + 128]
                bottom = pltpu.roll(g[CH:, rnd * 128 : rnd * 128 + 128], CH, 1)
                start = pl.multiple_of(((rnd * 2 + b) * FC + f) * CH, CH)
                res[pl.ds(start, CH), :] = bottom + sign * top
        return carry

    lax.fori_loop(0, FC, one_bin, 0, unroll=2)
    for r in range(8):
        dst = (z + r) & 7
        for crel in range(2):
            row = ((dst >> 1) * 2 + (c ^ crel)) * 8
            for rnd in range(2):
                base = (rnd * 2 + (dst & 1)) * FC * CH + row
                for i in range(8):
                    outs[r][crel, rnd, i] = res[pl.ds(base + i, FC, stride=CH), :].astype(BF16)


def cross(own0, own1, prev0, prev1, pos, *after):
    shape = jax.ShapeDtypeStruct((2, 2, 8, FC, 128), BF16)
    return pl.pallas_call(
        cross_kernel,
        out_shape=[shape] * 8,
        in_specs=[SM] + [VM] * 4 + [ANY] * len(after),
        out_specs=[VM] * 8,
        scratch_shapes=[
            pltpu.VMEM((32 * WIN * FC, 128), F32),
            pltpu.VMEM((4 * FC * CH, 128), F32),
        ],
        compiler_params=params(),
        cost_estimate=pl.CostEstimate(
            flops=4 * FC * 128 * 256 * 256, bytes_accessed=3 << 20, transcendentals=0
        ),
        name="cross",
    )(pos, own0, own1, prev0, prev1, *after)


def turn_kernel(pos_ref, *refs):
    ins, (same, other, buf) = refs[:8], refs[-3:]
    z = pos_ref[0]
    for crel, out in enumerate((same, other)):
        for rnd in range(2):
            for i in range(8):
                for r in range(8):
                    start = pl.multiple_of(((z - r) & 7) * FC, FC)
                    buf[pl.ds(start, FC), :] = ins[r][crel, rnd, i].astype(F32)
                out[rnd, i] = buf[...].T.astype(BF16)


def turn(pieces, pos, *after):
    shape = jax.ShapeDtypeStruct((2, 8, 128, 8 * FC), BF16)
    return pl.pallas_call(
        turn_kernel,
        out_shape=[shape] * 2,
        in_specs=[SM] + [VM] * 8 + [ANY] * len(after),
        out_specs=[VM] * 2,
        scratch_shapes=[pltpu.VMEM((8 * FC, 128), F32)],
        compiler_params=params(),
        cost_estimate=pl.CostEstimate(flops=0, bytes_accessed=4 << 20, transcendentals=0),
        name="turn",
    )(pos, *pieces, *after)


def invert_kernel(scaling, *refs):
    parts, (table, out) = refs[: 2 * CHUNKS], refs[2 * CHUNKS :]
    rows = []
    for i in range(4):
        cols = [p[0, i, k * CH : (k + 1) * CH] for k in range(2) for p in parts]
        rows.append(jnp.concatenate(cols, axis=1))
    left = jnp.concatenate(rows, axis=0)
    result = jnp.dot(left, table[...], preferred_element_type=F32) * scaling
    out[0] = result.reshape(4, CH, LAG_COUNT).astype(BF16)


def invert(parts, table, scaling):
    part = pl.BlockSpec((1, 4, 128, 8 * FC), lambda r, i: (r, i, 0, 0))
    return pl.pallas_call(
        functools.partial(invert_kernel, scaling),
        out_shape=jax.ShapeDtypeStruct((2, 8, CH, LAG_COUNT), BF16),
        grid=(2, 2),
        in_specs=[part] * (2 * CHUNKS) + [pl.BlockSpec((2 * BINS, LAG_COUNT), lambda r, i: (0, 0))],
        out_specs=pl.BlockSpec((1, 4, CH, LAG_COUNT), lambda r, i: (r, i, 0, 0)),
        compiler_params=params(),
        cost_estimate=pl.CostEstimate(
            flops=2 * 1024 * 1024 * 1024, bytes_accessed=6 << 20, transcendentals=0
        ),
        name="invert",
    )(*parts, table)


def lag_table(core):
    n = lax.broadcasted_iota(jnp.int32, (BINS, LAG_COUNT), 0)
    fine = n % FC
    z = (n // FC) % 8
    part = (n // (8 * FC)) % 2
    chunk = n // (16 * FC)
    freq_ids = chunk * CBINS + z * (2 * FC) + (part ^ core) * FC + fine + BAND_START
    delay_ids = lax.broadcasted_iota(jnp.int32, (BINS, LAG_COUNT), 1) - LAG_COUNT // 2
    angles = jnp.mod(freq_ids * delay_ids, WIN_SAMPLES).astype(F32) * (2.0 * math.pi / WIN_SAMPLES)
    return jnp.concatenate([jnp.cos(angles), -jnp.sin(angles)], axis=0).astype(BF16)


def place(z):
    return (z % 2) * 4 + z // 2


def ring(value, shift):
    return lax.ppermute(
        value, ("zl", "zh"), [(place(z), place((z + shift) % 8)) for z in range(8)]
    )


def other_core(value):
    return lax.ppermute(value, "c", [(0, 1), (1, 0)])


ORDER = (4, 3, 5, 2, 6, 1, 7)


def round_ring(pieces):
    got = {0: pieces[0]}
    for r in ORDER:
        got[r] = ring(pieces[r], r)
    return [got[r] for r in range(8)]


def shards(spectra, valid_flags):
    z = 2 * lax.axis_index("zh") + lax.axis_index("zl")
    pos = jnp.stack([z, lax.axis_index("c")]).astype(jnp.int32)
    windows = spectra.shape[0] * lax.axis_size(("zh", "c"))
    scaling = 1.0 / math.sqrt(windows * BINS)
    flags = valid_flags.astype(F32)
    flags2 = jnp.concatenate([flags, flags], axis=1)[:, None, :]
    white = whiten(jnp.transpose(spectra, (2, 0, 1, 3)), flags2, pos)
    up = [(i, (i + 1) % 16) for i in range(16)]
    swap = [(2 * i + k, 2 * j + 1 - k) for i, j in up for k in range(2)]
    parts = []
    table = None
    crossed, turned = (), ()
    for k in range(CHUNKS):
        got = round_ring(white[k * 8 : k * 8 + 8])
        same, other, core = merge(got, pos, *(() if table is None else (table,)))
        prev0 = lax.ppermute(same, ("x", "y"), up)
        prev1 = lax.ppermute(other, ("x", "y", "c"), swap)
        own1 = other_core(other)
        if k == 0:
            table = lag_table(core[0])
        out = cross(same, own1, prev0, prev1, pos, *crossed)
        crossed = (out[0],)
        same, other = turn(round_ring(out), pos, *turned)
        turned = (same,)
        parts += [same, other_core(other)]
    return invert(parts, table, scaling)


def solution(mesh):
    grid = mesh.devices.reshape(4, 4, 2, 4, 2)
    fine = Mesh(grid, ("x", "y", "zl", "zh", "c"))
    blk, seg = ("x", "y", "zl"), ("zh", "c")
    in_specs = (P(seg, blk, None, None), P(seg, blk))
    out_specs = P(None, blk + seg, None, None)


    return jax.shard_map(shards, mesh=fine, in_specs=in_specs, out_specs=out_specs, check_vma=False)
```

```python
import functools
import math

import jax
import jax.numpy as jnp
from jax import lax
from jax.experimental import pallas as pl
from jax.experimental.pallas import tpu as pltpu
from jax.sharding import Mesh, PartitionSpec as P


LAG_COUNT = 1024
WIN_SAMPLES = 15000
BAND_START = 30
SMOOTH_HALF = 32
BINS = 512
WIN = 14
CH = 64
CHUNKS = 2
FC = 32 // CHUNKS
CBINS = BINS // CHUNKS
ORDER = (0, 4, 3, 5, 2, 6, 1, 7)
F32 = jnp.float32
BF16 = jnp.bfloat16

VM = pl.BlockSpec(memory_space=pltpu.VMEM)
SM = pl.BlockSpec(memory_space=pltpu.SMEM)
ANY = pl.BlockSpec(memory_space=pl.ANY)


def params():
    return pltpu.CompilerParams(vmem_limit_bytes=48 << 20)


def whiten_kernel(pos_ref, spec_ref, flags_ref, *refs):
    outs = refs[: 8 * CHUNKS]
    band, eye, invc, white = refs[8 * CHUNKS :]
    w = pl.program_id(0)
    z, c = pos_ref[0], pos_ref[1]

    @pl.when(w == 0)
    def _():
        rows = lax.broadcasted_iota(jnp.int32, (BINS, BINS), 0)
        cols = lax.broadcasted_iota(jnp.int32, (BINS, BINS), 1)
        band[...] = jnp.where(jnp.abs(rows - cols) <= SMOOTH_HALF, 1.0, 0.0).astype(BF16)
        r2 = lax.broadcasted_iota(jnp.int32, (256, 256), 0)
        c2 = lax.broadcasted_iota(jnp.int32, (256, 256), 1)
        eye[...] = jnp.where(r2 == c2, 1.0, 0.0).astype(BF16)
        f = lax.broadcasted_iota(jnp.int32, (BINS, 128), 0)
        count = jnp.minimum(f + SMOOTH_HALF, BINS - 1) - jnp.maximum(f - SMOOTH_HALF, 0) + 1
        invc[...] = 1.0 / count.astype(F32)

    re16, im16 = spec_ref[0, 0], spec_ref[1, 0]
    re, im = re16.astype(F32), im16.astype(F32)
    amp = jnp.sqrt(re * re + im * im).astype(BF16)
    amp2 = jnp.concatenate([amp, amp], axis=0)
    both = jnp.concatenate([re16, im16], axis=0)
    nt = (((1,), (1,)), ((), ()))
    summed = lax.dot_general(band[...], amp2, nt, preferred_element_type=F32)
    scale = flags_ref[0] / (summed * invc[...] + 1e-05)
    for h in range(2):
        half = lax.dot_general(
            eye[...], both[:, h * 256 : (h + 1) * 256], nt, preferred_element_type=F32
        )
        white[h * 256 : (h + 1) * 256] = (half * scale[h * 256 : (h + 1) * 256]).astype(BF16)
    for k in range(CHUNKS):
        for r in range(8):
            base = k * CBINS + ((z + r) & 7) * (2 * FC)
            for crel in range(2):
                start = pl.multiple_of(base + (c ^ crel) * FC, FC)
                outs[k * 8 + r][crel, w] = white[pl.ds(start, FC), :]


def whiten(spec, flags2, pos):
    shape = jax.ShapeDtypeStruct((2, WIN, FC, 128), BF16)
    full = pl.BlockSpec((2, WIN, FC, 128), lambda w, *_: (0, 0, 0, 0))
    return pl.pallas_call(
        whiten_kernel,
        out_shape=[shape] * (8 * CHUNKS),
        grid_spec=pltpu.PrefetchScalarGridSpec(
            num_scalar_prefetch=1,
            grid=(WIN,),
            in_specs=[
                pl.BlockSpec((2, 1, CH, BINS), lambda w, *_: (0, w, 0, 0)),
                pl.BlockSpec((1, 1, 128), lambda w, *_: (w, 0, 0)),
            ],
            out_specs=[full] * (8 * CHUNKS),
            scratch_shapes=[
                pltpu.VMEM((BINS, BINS), BF16),
                pltpu.VMEM((256, 256), BF16),
                pltpu.VMEM((BINS, 128), F32),
                pltpu.VMEM((BINS, 128), BF16),
            ],
        ),
        compiler_params=params(),
        cost_estimate=pl.CostEstimate(
            flops=3 * 512 * 512 * 128 * WIN, bytes_accessed=4 << 20, transcendentals=0
        ),
        name="whiten",
    )(pos, spec, flags2)


def merge_kernel(pos_ref, *refs):
    ins, (same, other, core) = refs[:8], refs[-3:]
    z = pos_ref[0]
    core[0] = pos_ref[1]
    for n, r in enumerate(ORDER):
        src = (z - r) & 7
        same[src & 1, src >> 1] = ins[n][0]
        other[src & 1, src >> 1] = ins[n][1]


def merge(pieces, pos, *after):
    shape = jax.ShapeDtypeStruct((2, 4, WIN, FC, 128), BF16)
    return pl.pallas_call(
        merge_kernel,
        out_shape=[shape] * 2 + [jax.ShapeDtypeStruct((1,), jnp.int32)],
        in_specs=[SM] + [VM] * 8 + [ANY] * len(after),
        out_specs=[VM] * 2 + [SM],
        compiler_params=params(),
        cost_estimate=pl.CostEstimate(
            flops=0, bytes_accessed=4 * 8 * WIN * FC * 256, transcendentals=0
        ),
        name="merge",
    )(pos, *pieces, *after)


def cross_kernel(pos_ref, own0, own1, prev0, prev1, *refs):
    outs, (wide, res) = refs[-10:-2], refs[-2:]
    z, c = pos_ref[0], pos_ref[1]
    rows = 4 * WIN * FC
    for n, (first, second) in enumerate(((own0, own1), (prev0, prev1))):
        for b in range(2):
            base = (n * 2 + b) * 2 * rows
            wide[base : base + rows] = first[b].reshape(rows, 128).astype(F32)
            wide[base + rows : base + 2 * rows] = second[b].reshape(rows, 128).astype(F32)
    sign = jnp.where(lax.broadcasted_iota(jnp.int32, (CH, 128), 1) < CH, 1.0, -1.0).astype(F32)
    tn = (((0,), (0,)), ((), ()))

    def one_bin(f, carry):
        x = [
            wide[pl.ds(n * 2 * rows + f, 8 * WIN, stride=FC), :].astype(BF16) for n in range(4)
        ]
        own_a, own_b, prev_a, prev_b = x
        for b, (left, rights) in enumerate(
            ((own_a, (prev_b, prev_a)), (own_b, (own_a, prev_b)))
        ):
            g = lax.dot_general(
                left, jnp.concatenate(rights, axis=1), tn, preferred_element_type=F32
            )
            for rnd in range(2):
                top = g[:CH, rnd * 128 : rnd * 128 + 128]
                bottom = pltpu.roll(g[CH:, rnd * 128 : rnd * 128 + 128], CH, 1)
                start = pl.multiple_of(((rnd * 2 + b) * FC + f) * CH, CH)
                res[pl.ds(start, CH), :] = bottom + sign * top
        return carry

    lax.fori_loop(0, FC, one_bin, 0, unroll=2)
    for r in range(8):
        dst = (z + r) & 7
        for crel in range(2):
            row = ((dst >> 1) * 2 + (c ^ crel)) * 8
            for rnd in range(2):
                base = (rnd * 2 + (dst & 1)) * FC * CH + row
                for i in range(8):
                    outs[r][crel, rnd, i] = res[pl.ds(base + i, FC, stride=CH), :].astype(BF16)


def cross(own0, own1, prev0, prev1, pos, *after):
    shape = jax.ShapeDtypeStruct((2, 2, 8, FC, 128), BF16)
    return pl.pallas_call(
        cross_kernel,
        out_shape=[shape] * 8,
        in_specs=[SM] + [VM] * 4 + [ANY] * len(after),
        out_specs=[VM] * 8,
        scratch_shapes=[
            pltpu.VMEM((32 * WIN * FC, 128), F32),
            pltpu.VMEM((4 * FC * CH, 128), F32),
        ],
        compiler_params=params(),
        cost_estimate=pl.CostEstimate(
            flops=4 * FC * 128 * 256 * 256, bytes_accessed=3 << 20, transcendentals=0
        ),
        name="cross",
    )(pos, own0, own1, prev0, prev1, *after)


def turn_kernel(pos_ref, *refs):
    ins, (same, other, buf) = refs[:8], refs[-3:]
    z = pos_ref[0]
    for crel, out in enumerate((same, other)):
        for rnd in range(2):
            for i in range(8):
                for n, r in enumerate(ORDER):
                    start = pl.multiple_of(((z - r) & 7) * FC, FC)
                    buf[pl.ds(start, FC), :] = ins[n][crel, rnd, i].astype(F32)
                out[rnd, i] = buf[...].T.astype(BF16)


def turn(pieces, pos, *after):
    shape = jax.ShapeDtypeStruct((2, 8, 128, 8 * FC), BF16)
    return pl.pallas_call(
        turn_kernel,
        out_shape=[shape] * 2,
        in_specs=[SM] + [VM] * 8 + [ANY] * len(after),
        out_specs=[VM] * 2,
        scratch_shapes=[pltpu.VMEM((8 * FC, 128), F32)],
        compiler_params=params(),
        cost_estimate=pl.CostEstimate(flops=0, bytes_accessed=4 << 20, transcendentals=0),
        name="turn",
    )(pos, *pieces, *after)


def invert_kernel(scaling, *refs):
    parts, (table, out) = refs[: 2 * CHUNKS], refs[2 * CHUNKS :]
    rows = []
    for i in range(4):
        cols = [p[0, i, k * CH : (k + 1) * CH] for k in range(2) for p in parts]
        rows.append(jnp.concatenate(cols, axis=1))
    left = jnp.concatenate(rows, axis=0)
    result = jnp.dot(left, table[...], preferred_element_type=F32) * scaling
    out[0] = result.reshape(4, CH, LAG_COUNT).astype(BF16)


def invert(parts, table, scaling):
    part = pl.BlockSpec((1, 4, 128, 8 * FC), lambda r, i: (r, i, 0, 0))
    return pl.pallas_call(
        functools.partial(invert_kernel, scaling),
        out_shape=jax.ShapeDtypeStruct((2, 8, CH, LAG_COUNT), BF16),
        grid=(2, 2),
        in_specs=[part] * (2 * CHUNKS) + [pl.BlockSpec((2 * BINS, LAG_COUNT), lambda r, i: (0, 0))],
        out_specs=pl.BlockSpec((1, 4, CH, LAG_COUNT), lambda r, i: (r, i, 0, 0)),
        compiler_params=params(),
        cost_estimate=pl.CostEstimate(
            flops=2 * 1024 * 1024 * 1024, bytes_accessed=6 << 20, transcendentals=0
        ),
        name="invert",
    )(*parts, table)


def lag_table(core):
    n = lax.broadcasted_iota(jnp.int32, (BINS, LAG_COUNT), 0)
    fine = n % FC
    z = (n // FC) % 8
    part = (n // (8 * FC)) % 2
    chunk = n // (16 * FC)
    freq_ids = chunk * CBINS + z * (2 * FC) + (part ^ core) * FC + fine + BAND_START
    delay_ids = lax.broadcasted_iota(jnp.int32, (BINS, LAG_COUNT), 1) - LAG_COUNT // 2
    angles = jnp.mod(freq_ids * delay_ids, WIN_SAMPLES).astype(F32) * (2.0 * math.pi / WIN_SAMPLES)
    return jnp.concatenate([jnp.cos(angles), -jnp.sin(angles)], axis=0).astype(BF16)


def place(z):
    return (z % 2) * 4 + z // 2


def ring(value, shift):
    return lax.ppermute(
        value, ("zl", "zh"), [(place(z), place((z + shift) % 8)) for z in range(8)]
    )


def other_core(value):
    return lax.ppermute(value, "c", [(0, 1), (1, 0)])


def round_ring(pieces):
    return [ring(pieces[r], r) if r else pieces[0] for r in ORDER]


def shards(spectra, valid_flags):
    z = 2 * lax.axis_index("zh") + lax.axis_index("zl")
    pos = jnp.stack([z, lax.axis_index("c")]).astype(jnp.int32)
    windows = spectra.shape[0] * lax.axis_size(("zh", "c"))
    scaling = 1.0 / math.sqrt(windows * BINS)
    flags = valid_flags.astype(F32)
    flags2 = jnp.concatenate([flags, flags], axis=1)[:, None, :]
    white = whiten(jnp.transpose(spectra, (2, 0, 1, 3)), flags2, pos)
    up = [(i, (i + 1) % 16) for i in range(16)]
    swap = [(2 * i + k, 2 * j + 1 - k) for i, j in up for k in range(2)]
    parts = []
    table = None
    crossed, turned = (), ()
    for k in range(CHUNKS):
        got = round_ring(white[k * 8 : k * 8 + 8])
        same, other, core = merge(got, pos, *(() if table is None else (table,)))
        prev0 = lax.ppermute(same, ("x", "y"), up)
        prev1 = lax.ppermute(other, ("x", "y", "c"), swap)
        own1 = other_core(other)
        if k == 0:
            table = lag_table(core[0])
        out = cross(same, own1, prev0, prev1, pos, *crossed)
        crossed = (out[0],)
        same, other = turn(round_ring(out), pos, *turned)
        turned = (same,)
        parts += [same, other_core(other)]
    return invert(parts, table, scaling)


def solution(mesh):
    grid = mesh.devices.reshape(4, 4, 2, 4, 2)
    fine = Mesh(grid, ("x", "y", "zl", "zh", "c"))
    blk, seg = ("x", "y", "zl"), ("zh", "c")
    in_specs = (P(seg, blk, None, None), P(seg, blk))
    out_specs = P(None, blk + seg, None, None)


    return jax.shard_map(shards, mesh=fine, in_specs=in_specs, out_specs=out_specs, check_vma=False)
```

```python
import functools
import math

import jax
import jax.numpy as jnp
from jax import lax
from jax.experimental import pallas as pl
from jax.experimental.pallas import tpu as pltpu
from jax.sharding import Mesh, PartitionSpec as P


LAG_COUNT = 1024
WIN_SAMPLES = 15000
BAND_START = 30
SMOOTH_HALF = 32
BINS = 512
WIN = 14
CH = 64
CHUNKS = 2
FC = 32 // CHUNKS
CBINS = BINS // CHUNKS
ORDER = (0, 4, 3, 5, 2, 6, 1, 7)
F32 = jnp.float32
BF16 = jnp.bfloat16

VM = pl.BlockSpec(memory_space=pltpu.VMEM)
SM = pl.BlockSpec(memory_space=pltpu.SMEM)
ANY = pl.BlockSpec(memory_space=pl.ANY)


def params():
    return pltpu.CompilerParams(vmem_limit_bytes=48 << 20)


def whiten_kernel(pos_ref, spec_ref, flags_ref, *refs):
    outs = refs[: 8 * CHUNKS]
    band, eye, invc, white = refs[8 * CHUNKS :]
    w = pl.program_id(0)
    z, c = pos_ref[0], pos_ref[1]

    @pl.when(w == 0)
    def _():
        rows = lax.broadcasted_iota(jnp.int32, (BINS, BINS), 0)
        cols = lax.broadcasted_iota(jnp.int32, (BINS, BINS), 1)
        band[...] = jnp.where(jnp.abs(rows - cols) <= SMOOTH_HALF, 1.0, 0.0).astype(BF16)
        r2 = lax.broadcasted_iota(jnp.int32, (256, 256), 0)
        c2 = lax.broadcasted_iota(jnp.int32, (256, 256), 1)
        eye[...] = jnp.where(r2 == c2, 1.0, 0.0).astype(BF16)
        f = lax.broadcasted_iota(jnp.int32, (BINS, 128), 0)
        count = jnp.minimum(f + SMOOTH_HALF, BINS - 1) - jnp.maximum(f - SMOOTH_HALF, 0) + 1
        invc[...] = 1.0 / count.astype(F32)

    re16, im16 = spec_ref[0, 0], spec_ref[1, 0]
    re, im = re16.astype(F32), im16.astype(F32)
    amp = jnp.sqrt(re * re + im * im).astype(BF16)
    amp2 = jnp.concatenate([amp, amp], axis=0)
    both = jnp.concatenate([re16, im16], axis=0)
    nt = (((1,), (1,)), ((), ()))
    summed = lax.dot_general(band[...], amp2, nt, preferred_element_type=F32)
    scale = flags_ref[0].astype(F32) / (summed * invc[...] + 1e-05)
    for h in range(2):
        half = lax.dot_general(
            eye[...], both[:, h * 256 : (h + 1) * 256], nt, preferred_element_type=F32
        )
        white[h * 256 : (h + 1) * 256] = (half * scale[h * 256 : (h + 1) * 256]).astype(BF16)
    for k in range(CHUNKS):
        for r in range(8):
            base = k * CBINS + ((z + r) & 7) * (2 * FC)
            for crel in range(2):
                start = pl.multiple_of(base + (c ^ crel) * FC, FC)
                outs[k * 8 + r][crel, w] = white[pl.ds(start, FC), :]


def whiten(spec, flags2, pos):
    shape = jax.ShapeDtypeStruct((2, WIN, FC, 128), BF16)
    full = pl.BlockSpec((2, WIN, FC, 128), lambda w, *_: (0, 0, 0, 0))
    return pl.pallas_call(
        whiten_kernel,
        out_shape=[shape] * (8 * CHUNKS),
        grid_spec=pltpu.PrefetchScalarGridSpec(
            num_scalar_prefetch=1,
            grid=(WIN,),
            in_specs=[
                pl.BlockSpec((2, 1, CH, BINS), lambda w, *_: (0, w, 0, 0)),
                pl.BlockSpec((1, 1, 128), lambda w, *_: (w, 0, 0)),
            ],
            out_specs=[full] * (8 * CHUNKS),
            scratch_shapes=[
                pltpu.VMEM((BINS, BINS), BF16),
                pltpu.VMEM((256, 256), BF16),
                pltpu.VMEM((BINS, 128), F32),
                pltpu.VMEM((BINS, 128), BF16),
            ],
        ),
        compiler_params=params(),
        cost_estimate=pl.CostEstimate(
            flops=3 * 512 * 512 * 128 * WIN, bytes_accessed=4 << 20, transcendentals=0
        ),
        name="whiten",
    )(pos, spec, flags2)


def merge_kernel(pos_ref, *refs):
    ins, (same, other, core) = refs[:8], refs[-3:]
    z = pos_ref[0]
    core[0] = pos_ref[1]
    for n, r in enumerate(ORDER):
        src = (z - r) & 7
        same[src & 1, src >> 1] = ins[n][0]
        other[src & 1, src >> 1] = ins[n][1]


def merge(pieces, pos, *after):
    shape = jax.ShapeDtypeStruct((2, 4, WIN, FC, 128), BF16)
    return pl.pallas_call(
        merge_kernel,
        out_shape=[shape] * 2 + [jax.ShapeDtypeStruct((1,), jnp.int32)],
        in_specs=[SM] + [VM] * 8 + [ANY] * len(after),
        out_specs=[VM] * 2 + [SM],
        compiler_params=params(),
        cost_estimate=pl.CostEstimate(
            flops=0, bytes_accessed=4 * 8 * WIN * FC * 256, transcendentals=0
        ),
        name="merge",
    )(pos, *pieces, *after)


def cross_kernel(pos_ref, own0, own1, prev0, prev1, *refs):
    outs, (wide, res) = refs[-10:-2], refs[-2:]
    z, c = pos_ref[0], pos_ref[1]
    rows = 4 * WIN * FC
    for n, (first, second) in enumerate(((own0, own1), (prev0, prev1))):
        for b in range(2):
            base = (n * 2 + b) * 2 * rows
            wide[base : base + rows] = first[b].reshape(rows, 128).astype(F32)
            wide[base + rows : base + 2 * rows] = second[b].reshape(rows, 128).astype(F32)
    sign = jnp.where(lax.broadcasted_iota(jnp.int32, (CH, 128), 1) < CH, 1.0, -1.0).astype(F32)
    tn = (((0,), (0,)), ((), ()))

    def one_bin(f, carry):
        x = [
            wide[pl.ds(n * 2 * rows + f, 8 * WIN, stride=FC), :].astype(BF16) for n in range(4)
        ]
        own_a, own_b, prev_a, prev_b = x
        for b, (left, rights) in enumerate(
            ((own_a, (prev_b, prev_a)), (own_b, (own_a, prev_b)))
        ):
            g = lax.dot_general(
                left, jnp.concatenate(rights, axis=1), tn, preferred_element_type=F32
            )
            for rnd in range(2):
                top = g[:CH, rnd * 128 : rnd * 128 + 128]
                bottom = pltpu.roll(g[CH:, rnd * 128 : rnd * 128 + 128], CH, 1)
                start = pl.multiple_of(((rnd * 2 + b) * FC + f) * CH, CH)
                res[pl.ds(start, CH), :] = bottom + sign * top
        return carry

    lax.fori_loop(0, FC, one_bin, 0, unroll=2)
    for r in range(8):
        dst = (z + r) & 7
        for crel in range(2):
            row = ((dst >> 1) * 2 + (c ^ crel)) * 8
            for rnd in range(2):
                base = (rnd * 2 + (dst & 1)) * FC * CH + row
                for i in range(8):
                    outs[r][crel, rnd, i] = res[pl.ds(base + i, FC, stride=CH), :].astype(BF16)


def cross(own0, own1, prev0, prev1, pos, *after):
    shape = jax.ShapeDtypeStruct((2, 2, 8, FC, 128), BF16)
    return pl.pallas_call(
        cross_kernel,
        out_shape=[shape] * 8,
        in_specs=[SM] + [VM] * 4 + [ANY] * len(after),
        out_specs=[VM] * 8,
        scratch_shapes=[
            pltpu.VMEM((32 * WIN * FC, 128), F32),
            pltpu.VMEM((4 * FC * CH, 128), F32),
        ],
        compiler_params=params(),
        cost_estimate=pl.CostEstimate(
            flops=4 * FC * 128 * 256 * 256, bytes_accessed=3 << 20, transcendentals=0
        ),
        name="cross",
    )(pos, own0, own1, prev0, prev1, *after)


def turn_kernel(pos_ref, *refs):
    ins, (same, other, buf) = refs[:8], refs[-3:]
    z = pos_ref[0]
    for crel, out in enumerate((same, other)):
        for rnd in range(2):
            for i in range(8):
                for n, r in enumerate(ORDER):
                    start = pl.multiple_of(((z - r) & 7) * FC, FC)
                    buf[pl.ds(start, FC), :] = ins[n][crel, rnd, i].astype(F32)
                out[rnd, i] = buf[...].T.astype(BF16)


def turn(pieces, pos, *after):
    shape = jax.ShapeDtypeStruct((2, 8, 128, 8 * FC), BF16)
    return pl.pallas_call(
        turn_kernel,
        out_shape=[shape] * 2,
        in_specs=[SM] + [VM] * 8 + [ANY] * len(after),
        out_specs=[VM] * 2,
        scratch_shapes=[pltpu.VMEM((8 * FC, 128), F32)],
        compiler_params=params(),
        cost_estimate=pl.CostEstimate(flops=0, bytes_accessed=4 << 20, transcendentals=0),
        name="turn",
    )(pos, *pieces, *after)


def invert_kernel(scaling, *refs):
    parts, (table, out) = refs[: 2 * CHUNKS], refs[2 * CHUNKS :]
    rows = []
    for i in range(4):
        cols = [p[0, i, k * CH : (k + 1) * CH] for k in range(2) for p in parts]
        rows.append(jnp.concatenate(cols, axis=1))
    left = jnp.concatenate(rows, axis=0)
    result = jnp.dot(left, table[...], preferred_element_type=F32) * scaling
    out[0] = result.reshape(4, CH, LAG_COUNT).astype(BF16)


def invert(parts, table, scaling):
    part = pl.BlockSpec((1, 4, 128, 8 * FC), lambda r, i: (r, i, 0, 0))
    return pl.pallas_call(
        functools.partial(invert_kernel, scaling),
        out_shape=jax.ShapeDtypeStruct((2, 8, CH, LAG_COUNT), BF16),
        grid=(2, 2),
        in_specs=[part] * (2 * CHUNKS) + [pl.BlockSpec((2 * BINS, LAG_COUNT), lambda r, i: (0, 0))],
        out_specs=pl.BlockSpec((1, 4, CH, LAG_COUNT), lambda r, i: (r, i, 0, 0)),
        compiler_params=params(),
        cost_estimate=pl.CostEstimate(
            flops=2 * 1024 * 1024 * 1024, bytes_accessed=6 << 20, transcendentals=0
        ),
        name="invert",
    )(*parts, table)


def lag_table(core):
    n = lax.broadcasted_iota(jnp.int32, (BINS, LAG_COUNT), 0)
    fine = n % FC
    z = (n // FC) % 8
    part = (n // (8 * FC)) % 2
    chunk = n // (16 * FC)
    freq_ids = chunk * CBINS + z * (2 * FC) + (part ^ core) * FC + fine + BAND_START
    delay_ids = lax.broadcasted_iota(jnp.int32, (BINS, LAG_COUNT), 1) - LAG_COUNT // 2
    angles = jnp.mod(freq_ids * delay_ids, WIN_SAMPLES).astype(F32) * (2.0 * math.pi / WIN_SAMPLES)
    return jnp.concatenate([jnp.cos(angles), -jnp.sin(angles)], axis=0).astype(BF16)


def place(z):
    return (z % 2) * 4 + z // 2


def ring(value, shift):
    return lax.ppermute(
        value, ("zl", "zh"), [(place(z), place((z + shift) % 8)) for z in range(8)]
    )


def other_core(value):
    return lax.ppermute(value, "c", [(0, 1), (1, 0)])


def round_ring(pieces):
    got = []
    for r in ORDER:
        got.append(ring(pieces[r], r) if r else pieces[0])
    return got


def shards(spectra, valid_flags):
    z = 2 * lax.axis_index("zh") + lax.axis_index("zl")
    pos = jnp.stack([z, lax.axis_index("c")]).astype(jnp.int32)
    windows = spectra.shape[0] * lax.axis_size(("zh", "c"))
    scaling = 1.0 / math.sqrt(windows * BINS)
    flags2 = jnp.concatenate([valid_flags, valid_flags], axis=1)[:, None, :]
    white = whiten(jnp.transpose(spectra, (2, 0, 1, 3)), flags2, pos)
    up = [(i, (i + 1) % 16) for i in range(16)]
    swap = [(2 * i + k, 2 * j + 1 - k) for i, j in up for k in range(2)]
    parts = []
    table = None
    crossed, turned = (), ()
    for k in range(CHUNKS):
        got = round_ring(white[k * 8 : k * 8 + 8])
        same, other, core = merge(got, pos, *(() if table is None else (table,)))
        prev0 = lax.ppermute(same, ("x", "y"), up)
        prev1 = lax.ppermute(other, ("x", "y", "c"), swap)
        own1 = other_core(other)
        if k == 0:
            table = lag_table(core[0])
        out = cross(same, own1, prev0, prev1, pos, *crossed)
        crossed = (out[0],)
        same, other = turn(round_ring(out), pos, *turned)
        turned = (same,)
        parts += [same, other_core(other)]
    return invert(parts, table, scaling)


def solution(mesh):
    grid = mesh.devices.reshape(4, 4, 2, 4, 2)
    fine = Mesh(grid, ("x", "y", "zl", "zh", "c"))
    blk, seg = ("x", "y", "zl"), ("zh", "c")
    in_specs = (P(seg, blk, None, None), P(seg, blk))
    out_specs = P(None, blk + seg, None, None)


    return jax.shard_map(shards, mesh=fine, in_specs=in_specs, out_specs=out_specs, check_vma=False)
```

```python
import functools
import math

import jax
import jax.numpy as jnp
from jax import lax
from jax.experimental import pallas as pl
from jax.experimental.pallas import tpu as pltpu
from jax.sharding import Mesh, PartitionSpec as P


LAG_COUNT = 1024
WIN_SAMPLES = 15000
BAND_START = 30
SMOOTH_HALF = 32
BINS = 512
WIN = 14
CH = 64
CHUNKS = 2
FC = 32 // CHUNKS
CBINS = BINS // CHUNKS
ORDER = (0, 4, 3, 5, 2, 6, 1, 7)
F32 = jnp.float32
BF16 = jnp.bfloat16

ALL = ("x", "y", "zl", "zh", "c")
VM = pl.BlockSpec(memory_space=pltpu.VMEM)
SM = pl.BlockSpec(memory_space=pltpu.SMEM)
ANY = pl.BlockSpec(memory_space=pl.ANY)


def params():
    return pltpu.CompilerParams(vmem_limit_bytes=48 << 20)


def whiten_kernel(pos_ref, spec_ref, flags_ref, *refs):
    outs = refs[: 8 * CHUNKS]
    band, eye, invc, white = refs[8 * CHUNKS :]
    w = pl.program_id(0)
    z, c = pos_ref[0], pos_ref[1]

    @pl.when(w == 0)
    def _():
        rows = lax.broadcasted_iota(jnp.int32, (BINS, BINS), 0)
        cols = lax.broadcasted_iota(jnp.int32, (BINS, BINS), 1)
        band[...] = jnp.where(jnp.abs(rows - cols) <= SMOOTH_HALF, 1.0, 0.0).astype(BF16)
        r2 = lax.broadcasted_iota(jnp.int32, (256, 256), 0)
        c2 = lax.broadcasted_iota(jnp.int32, (256, 256), 1)
        eye[...] = jnp.where(r2 == c2, 1.0, 0.0).astype(BF16)
        f = lax.broadcasted_iota(jnp.int32, (BINS, 128), 0)
        count = jnp.minimum(f + SMOOTH_HALF, BINS - 1) - jnp.maximum(f - SMOOTH_HALF, 0) + 1
        invc[...] = 1.0 / count.astype(F32)

    re16, im16 = spec_ref[0, 0], spec_ref[1, 0]
    re, im = re16.astype(F32), im16.astype(F32)
    amp = jnp.sqrt(re * re + im * im).astype(BF16)
    amp2 = jnp.concatenate([amp, amp], axis=0)
    both = jnp.concatenate([re16, im16], axis=0)
    nt = (((1,), (1,)), ((), ()))
    summed = lax.dot_general(band[...], amp2, nt, preferred_element_type=F32)
    scale = flags_ref[0].astype(F32) / (summed * invc[...] + 1e-05)
    for h in range(2):
        half = lax.dot_general(
            eye[...], both[:, h * 256 : (h + 1) * 256], nt, preferred_element_type=F32
        )
        white[h * 256 : (h + 1) * 256] = (half * scale[h * 256 : (h + 1) * 256]).astype(BF16)
    for k in range(CHUNKS):
        for r in range(8):
            base = k * CBINS + ((z + r) & 7) * (2 * FC)
            for crel in range(2):
                start = pl.multiple_of(base + (c ^ crel) * FC, FC)
                outs[k * 8 + r][crel, w] = white[pl.ds(start, FC), :]


def whiten(spec, flags2, pos):
    shape = jax.ShapeDtypeStruct((2, WIN, FC, 128), BF16)
    full = pl.BlockSpec((2, WIN, FC, 128), lambda w, *_: (0, 0, 0, 0))
    return pl.pallas_call(
        whiten_kernel,
        out_shape=[shape] * (8 * CHUNKS),
        grid_spec=pltpu.PrefetchScalarGridSpec(
            num_scalar_prefetch=1,
            grid=(WIN,),
            in_specs=[
                pl.BlockSpec((2, 1, CH, BINS), lambda w, *_: (0, w, 0, 0)),
                pl.BlockSpec((1, 1, 128), lambda w, *_: (w, 0, 0)),
            ],
            out_specs=[full] * (8 * CHUNKS),
            scratch_shapes=[
                pltpu.VMEM((BINS, BINS), BF16),
                pltpu.VMEM((256, 256), BF16),
                pltpu.VMEM((BINS, 128), F32),
                pltpu.VMEM((BINS, 128), BF16),
            ],
        ),
        compiler_params=params(),
        cost_estimate=pl.CostEstimate(
            flops=3 * 512 * 512 * 128 * WIN, bytes_accessed=4 << 20, transcendentals=0
        ),
        name="whiten",
    )(pos, spec, flags2)


def merge_kernel(pos_ref, *refs):
    ins, (same, other, core) = refs[:8], refs[-3:]
    z = pos_ref[0]
    core[0] = pos_ref[1]
    for n, r in enumerate(ORDER):
        src = (z - r) & 7
        same[src & 1, src >> 1] = ins[n][0]
        other[src & 1, src >> 1] = ins[n][1]


def merge(pieces, pos, *after):
    shape = jax.ShapeDtypeStruct((2, 4, WIN, FC, 128), BF16)
    return pl.pallas_call(
        merge_kernel,
        out_shape=[shape] * 2 + [jax.ShapeDtypeStruct((1,), jnp.int32)],
        in_specs=[SM] + [VM] * 8 + [ANY] * len(after),
        out_specs=[VM] * 2 + [SM],
        compiler_params=params(),
        cost_estimate=pl.CostEstimate(
            flops=0, bytes_accessed=4 * 8 * WIN * FC * 256, transcendentals=0
        ),
        name="merge",
    )(pos, *pieces, *after)


def cross_kernel(pos_ref, own0, own1, prev0, prev1, *refs):
    outs, (wide, res) = refs[-10:-2], refs[-2:]
    z, c = pos_ref[0], pos_ref[1]
    rows = 4 * WIN * FC
    for n, (first, second) in enumerate(((own0, own1), (prev0, prev1))):
        for b in range(2):
            base = pl.multiple_of(((n ^ c) * 2 + b) * 2 * rows, rows)
            wide[pl.ds(base, rows)] = first[b].reshape(rows, 128).astype(F32)
            wide[pl.ds(base + rows, rows)] = second[b].reshape(rows, 128).astype(F32)
    sign = jnp.where(lax.broadcasted_iota(jnp.int32, (CH, 128), 1) < CH, 1.0, -1.0).astype(F32)
    tn = (((0,), (0,)), ((), ()))

    def one_bin(f, carry):
        x = [
            wide[pl.ds(n * 2 * rows + f, 8 * WIN, stride=FC), :].astype(BF16) for n in range(4)
        ]
        own_a, own_b, prev_a, prev_b = x
        for b, (left, rights) in enumerate(
            ((own_a, (prev_b, prev_a)), (own_b, (own_a, prev_b)))
        ):
            g = lax.dot_general(
                left, jnp.concatenate(rights, axis=1), tn, preferred_element_type=F32
            )
            for rnd in range(2):
                top = g[:CH, rnd * 128 : rnd * 128 + 128]
                bottom = pltpu.roll(g[CH:, rnd * 128 : rnd * 128 + 128], CH, 1)
                start = pl.multiple_of(((rnd * 2 + b) * FC + f) * CH, CH)
                res[pl.ds(start, CH), :] = bottom + sign * top
        return carry

    lax.fori_loop(0, FC, one_bin, 0, unroll=2)
    for r in range(8):
        dst = (z + r) & 7
        for crel in range(2):
            row = ((dst >> 1) * 2 + (c ^ crel)) * 8
            for rnd in range(2):
                base = (rnd * 2 + (dst & 1)) * FC * CH + row
                for i in range(8):
                    outs[r][crel, rnd, i] = res[pl.ds(base + i, FC, stride=CH), :].astype(BF16)


def cross(own0, own1, prev0, prev1, pos, *after):
    shape = jax.ShapeDtypeStruct((2, 2, 8, FC, 128), BF16)
    return pl.pallas_call(
        cross_kernel,
        out_shape=[shape] * 8,
        in_specs=[SM] + [VM] * 4 + [ANY] * len(after),
        out_specs=[VM] * 8,
        scratch_shapes=[
            pltpu.VMEM((32 * WIN * FC, 128), F32),
            pltpu.VMEM((4 * FC * CH, 128), F32),
        ],
        compiler_params=params(),
        cost_estimate=pl.CostEstimate(
            flops=4 * FC * 128 * 256 * 256, bytes_accessed=3 << 20, transcendentals=0
        ),
        name="cross",
    )(pos, own0, own1, prev0, prev1, *after)


def turn_kernel(pos_ref, *refs):
    ins, (same, other, buf) = refs[:8], refs[-3:]
    z = pos_ref[0]
    for crel, out in enumerate((same, other)):
        for rnd in range(2):
            for i in range(8):
                for n, r in enumerate(ORDER):
                    start = pl.multiple_of(((z - r) & 7) * FC, FC)
                    buf[pl.ds(start, FC), :] = ins[n][crel, rnd, i].astype(F32)
                out[rnd, i] = buf[...].T.astype(BF16)


def turn(pieces, pos, *after):
    shape = jax.ShapeDtypeStruct((2, 8, 128, 8 * FC), BF16)
    return pl.pallas_call(
        turn_kernel,
        out_shape=[shape] * 2,
        in_specs=[SM] + [VM] * 8 + [ANY] * len(after),
        out_specs=[VM] * 2,
        scratch_shapes=[pltpu.VMEM((8 * FC, 128), F32)],
        compiler_params=params(),
        cost_estimate=pl.CostEstimate(flops=0, bytes_accessed=4 << 20, transcendentals=0),
        name="turn",
    )(pos, *pieces, *after)


def invert_kernel(scaling, *refs):
    parts, (table, out) = refs[: 2 * CHUNKS], refs[2 * CHUNKS :]
    rows = []
    for i in range(4):
        cols = [p[0, i, k * CH : (k + 1) * CH] for k in range(2) for p in parts]
        rows.append(jnp.concatenate(cols, axis=1))
    left = jnp.concatenate(rows, axis=0)
    result = jnp.dot(left, table[...], preferred_element_type=F32) * scaling
    out[0] = result.reshape(4, CH, LAG_COUNT).astype(BF16)


def invert(parts, table, scaling):
    part = pl.BlockSpec((1, 4, 128, 8 * FC), lambda r, i: (r, i, 0, 0))
    return pl.pallas_call(
        functools.partial(invert_kernel, scaling),
        out_shape=jax.ShapeDtypeStruct((2, 8, CH, LAG_COUNT), BF16),
        grid=(2, 2),
        in_specs=[part] * (2 * CHUNKS) + [pl.BlockSpec((2 * BINS, LAG_COUNT), lambda r, i: (0, 0))],
        out_specs=pl.BlockSpec((1, 4, CH, LAG_COUNT), lambda r, i: (r, i, 0, 0)),
        compiler_params=params(),
        cost_estimate=pl.CostEstimate(
            flops=2 * 1024 * 1024 * 1024, bytes_accessed=6 << 20, transcendentals=0
        ),
        name="invert",
    )(*parts, table)


def lag_table(core):
    n = lax.broadcasted_iota(jnp.int32, (BINS, LAG_COUNT), 0)
    fine = n % FC
    z = (n // FC) % 8
    part = (n // (8 * FC)) % 2
    chunk = n // (16 * FC)
    freq_ids = chunk * CBINS + z * (2 * FC) + (part ^ core) * FC + fine + BAND_START
    delay_ids = lax.broadcasted_iota(jnp.int32, (BINS, LAG_COUNT), 1) - LAG_COUNT // 2
    angles = jnp.mod(freq_ids * delay_ids, WIN_SAMPLES).astype(F32) * (2.0 * math.pi / WIN_SAMPLES)
    return jnp.concatenate([jnp.cos(angles), -jnp.sin(angles)], axis=0).astype(BF16)


def place(z):
    return (z % 2) * 4 + z // 2


def ring(value, r):
    pairs = [(place(z), place((z + r) % 8)) for z in range(8)]
    return lax.ppermute(value, ("zl", "zh"), pairs)


def device(m, z, c):
    return (m % 16) * 16 + place(z % 8) * 2 + c


EVERY = [(m, z, c) for m in range(16) for z in range(8) for c in range(2)]


def ring_back(value, r):
    pairs = [(device(m, z, c), device(m + c, z + r, c)) for m, z, c in EVERY]
    return lax.ppermute(value, ALL, pairs)


def round_ring(pieces, name):
    got = []
    for r in ORDER:
        if name == "back":
            got.append(ring_back(pieces[r], r))
        else:
            got.append(ring(pieces[r], r) if r else pieces[0])
    return got


def other_core(value):
    return lax.ppermute(value, "c", [(0, 1), (1, 0)])


def shards(spectra, valid_flags):
    z = 2 * lax.axis_index("zh") + lax.axis_index("zl")
    pos = jnp.stack([z, lax.axis_index("c")]).astype(jnp.int32)
    windows = spectra.shape[0] * lax.axis_size(("zh", "c"))
    scaling = 1.0 / math.sqrt(windows * BINS)
    flags2 = jnp.concatenate([valid_flags, valid_flags], axis=1)[:, None, :]
    white = whiten(jnp.transpose(spectra, (2, 0, 1, 3)), flags2, pos)
    keep = [(device(m, z, c), device(m + 1 - 2 * c, z, c)) for m, z, c in EVERY]
    swap = [(device(m, z, c), device(m - 1 + 2 * c, z, 1 - c)) for m, z, c in EVERY]
    parts = []
    table = None
    crossed, turned = (), ()
    for k in range(CHUNKS):
        got = round_ring(white[k * 8 : k * 8 + 8], "go")
        same, other, core = merge(got, pos, *(() if table is None else (table,)))
        prev0 = lax.ppermute(same, ALL, keep)
        prev1 = lax.ppermute(other, ALL, swap)
        own1 = other_core(other)
        if k == 0:
            table = lag_table(core[0])
        out = cross(same, own1, prev0, prev1, pos, *crossed)
        crossed = (out[0],)
        same, other = turn(round_ring(out, "back"), pos, *turned)
        turned = (same,)
        parts += [same, other_core(other)]
    return invert(parts, table, scaling)


def solution(mesh):
    grid = mesh.devices.reshape(4, 4, 2, 4, 2)
    fine = Mesh(grid, ("x", "y", "zl", "zh", "c"))
    blk, seg = ("x", "y", "zl"), ("zh", "c")
    in_specs = (P(seg, blk, None, None), P(seg, blk))
    out_specs = P(None, blk + seg, None, None)


    return jax.shard_map(shards, mesh=fine, in_specs=in_specs, out_specs=out_specs, check_vma=False)
```

```python
import functools
import math

import jax
import jax.numpy as jnp
from jax import lax
from jax.experimental import pallas as pl
from jax.experimental.pallas import tpu as pltpu
from jax.sharding import Mesh, PartitionSpec as P


LAG_COUNT = 1024
WIN_SAMPLES = 15000
BAND_START = 30
SMOOTH_HALF = 32
BINS = 512
WIN = 14
CH = 64
CHUNKS = 2
FC = 32 // CHUNKS
CBINS = BINS // CHUNKS
ORDER = (0, 4, 3, 5, 2, 6, 1, 7)
F32 = jnp.float32
BF16 = jnp.bfloat16

ALL = ("x", "y", "zl", "zh", "c")
VM = pl.BlockSpec(memory_space=pltpu.VMEM)
SM = pl.BlockSpec(memory_space=pltpu.SMEM)
ANY = pl.BlockSpec(memory_space=pl.ANY)


def place(z):
    return (z % 2) * 4 + z // 2


def params():
    return pltpu.CompilerParams(vmem_limit_bytes=48 << 20)


def whiten_kernel(pos_ref, spec_ref, flags_ref, *refs):
    outs, core, (band, eye, invc, white) = refs[:CHUNKS], refs[CHUNKS], refs[CHUNKS + 1 :]
    w = pl.program_id(0)

    @pl.when(w == 0)
    def _():
        rows = lax.broadcasted_iota(jnp.int32, (BINS, BINS), 0)
        cols = lax.broadcasted_iota(jnp.int32, (BINS, BINS), 1)
        band[...] = jnp.where(jnp.abs(rows - cols) <= SMOOTH_HALF, 1.0, 0.0).astype(BF16)
        r2 = lax.broadcasted_iota(jnp.int32, (256, 256), 0)
        c2 = lax.broadcasted_iota(jnp.int32, (256, 256), 1)
        eye[...] = jnp.where(r2 == c2, 1.0, 0.0).astype(BF16)
        f = lax.broadcasted_iota(jnp.int32, (BINS, 128), 0)
        count = jnp.minimum(f + SMOOTH_HALF, BINS - 1) - jnp.maximum(f - SMOOTH_HALF, 0) + 1
        invc[...] = 1.0 / count.astype(F32)

    re16, im16 = spec_ref[0, 0], spec_ref[1, 0]
    re, im = re16.astype(F32), im16.astype(F32)
    amp = jnp.sqrt(re * re + im * im).astype(BF16)
    amp2 = jnp.concatenate([amp, amp], axis=0)
    both = jnp.concatenate([re16, im16], axis=0)
    nt = (((1,), (1,)), ((), ()))
    summed = lax.dot_general(band[...], amp2, nt, preferred_element_type=F32)
    scale = flags_ref[0].astype(F32) / (summed * invc[...] + 1e-05)
    for h in range(2):
        half = lax.dot_general(
            eye[...], both[:, h * 256 : (h + 1) * 256], nt, preferred_element_type=F32
        )
        white[h * 256 : (h + 1) * 256] = (half * scale[h * 256 : (h + 1) * 256]).astype(BF16)
    for k in range(CHUNKS):
        for z in range(8):
            for c in range(2):
                start = k * CBINS + z * 2 * FC + c * FC
                outs[k][place(z) * 2 + c, w] = white[start : start + FC]
    core[0] = pos_ref[1]


def whiten(spec, flags2, pos):
    shape = jax.ShapeDtypeStruct((16, WIN, FC, 128), BF16)
    full = pl.BlockSpec((16, WIN, FC, 128), lambda w, *_: (0, 0, 0, 0))
    return pl.pallas_call(
        whiten_kernel,
        out_shape=[shape] * CHUNKS + [jax.ShapeDtypeStruct((1,), jnp.int32)],
        grid_spec=pltpu.PrefetchScalarGridSpec(
            num_scalar_prefetch=1,
            grid=(WIN,),
            in_specs=[
                pl.BlockSpec((2, 1, CH, BINS), lambda w, *_: (0, w, 0, 0)),
                pl.BlockSpec((1, 1, 128), lambda w, *_: (w, 0, 0)),
            ],
            out_specs=[full] * CHUNKS + [SM],
            scratch_shapes=[
                pltpu.VMEM((BINS, BINS), BF16),
                pltpu.VMEM((256, 256), BF16),
                pltpu.VMEM((BINS, 128), F32),
                pltpu.VMEM((BINS, 128), BF16),
            ],
        ),
        compiler_params=params(),
        cost_estimate=pl.CostEstimate(
            flops=3 * 512 * 512 * 128 * WIN, bytes_accessed=4 << 20, transcendentals=0
        ),
        name="whiten",
    )(pos, spec, flags2)


def cross_kernel(pos_ref, here, there, *refs):
    outs, (wide, res) = refs[-10:-2], refs[-2:]
    z, c = pos_ref[0], pos_ref[1]
    rows = 8 * WIN * FC
    for n, ref in enumerate((here, there)):
        for b in range(2):
            base = pl.multiple_of(((n ^ c) * 2 + b) * rows, rows)
            wide[pl.ds(base, rows)] = ref[8 * b : 8 * b + 8].reshape(rows, 128).astype(F32)
    sign = jnp.where(lax.broadcasted_iota(jnp.int32, (CH, 128), 1) < CH, 1.0, -1.0).astype(F32)
    tn = (((0,), (0,)), ((), ()))

    def one_bin(f, carry):
        x = [
            wide[pl.ds(n * rows + f, 8 * WIN, stride=FC), :].astype(BF16) for n in range(4)
        ]
        own_a, own_b, prev_a, prev_b = x
        for b, (left, rights) in enumerate(
            ((own_a, (prev_b, prev_a)), (own_b, (own_a, prev_b)))
        ):
            g = lax.dot_general(
                left, jnp.concatenate(rights, axis=1), tn, preferred_element_type=F32
            )
            for rnd in range(2):
                top = g[:CH, rnd * 128 : rnd * 128 + 128]
                bottom = pltpu.roll(g[CH:, rnd * 128 : rnd * 128 + 128], CH, 1)
                start = pl.multiple_of(((rnd * 2 + b) * FC + f) * CH, CH)
                res[pl.ds(start, CH), :] = bottom + sign * top
        return carry

    lax.fori_loop(0, FC, one_bin, 0, unroll=2)
    for r in range(8):
        dst = (z + r) & 7
        for crel in range(2):
            row = ((dst >> 1) * 2 + (c ^ crel)) * 8
            for rnd in range(2):
                base = (rnd * 2 + (dst & 1)) * FC * CH + row
                for i in range(8):
                    outs[r][crel, rnd, i] = res[pl.ds(base + i, FC, stride=CH), :].astype(BF16)


def cross(here, there, pos, *after):
    shape = jax.ShapeDtypeStruct((2, 2, 8, FC, 128), BF16)
    return pl.pallas_call(
        cross_kernel,
        out_shape=[shape] * 8,
        in_specs=[SM] + [VM] * 2 + [ANY] * len(after),
        out_specs=[VM] * 8,
        scratch_shapes=[
            pltpu.VMEM((32 * WIN * FC, 128), F32),
            pltpu.VMEM((4 * FC * CH, 128), F32),
        ],
        compiler_params=params(),
        cost_estimate=pl.CostEstimate(
            flops=4 * FC * 128 * 256 * 256, bytes_accessed=3 << 20, transcendentals=0
        ),
        name="cross",
    )(pos, here, there, *after)


def turn_kernel(pos_ref, *refs):
    ins, (same, other, buf) = refs[:8], refs[-3:]
    z = pos_ref[0]
    for crel, out in enumerate((same, other)):
        for rnd in range(2):
            for i in range(8):
                for n, r in enumerate(ORDER):
                    start = pl.multiple_of(((z - r) & 7) * FC, FC)
                    buf[pl.ds(start, FC), :] = ins[n][crel, rnd, i].astype(F32)
                out[rnd, i] = buf[...].T.astype(BF16)


def turn(pieces, pos, *after):
    shape = jax.ShapeDtypeStruct((2, 8, 128, 8 * FC), BF16)
    return pl.pallas_call(
        turn_kernel,
        out_shape=[shape] * 2,
        in_specs=[SM] + [VM] * 8 + [ANY] * len(after),
        out_specs=[VM] * 2,
        scratch_shapes=[pltpu.VMEM((8 * FC, 128), F32)],
        compiler_params=params(),
        cost_estimate=pl.CostEstimate(flops=0, bytes_accessed=4 << 20, transcendentals=0),
        name="turn",
    )(pos, *pieces, *after)


def invert_kernel(scaling, *refs):
    parts, (table, out) = refs[: 2 * CHUNKS], refs[2 * CHUNKS :]
    rows = []
    for i in range(4):
        cols = [p[0, i, k * CH : (k + 1) * CH] for k in range(2) for p in parts]
        rows.append(jnp.concatenate(cols, axis=1))
    left = jnp.concatenate(rows, axis=0)
    result = jnp.dot(left, table[...], preferred_element_type=F32) * scaling
    out[0] = result.reshape(4, CH, LAG_COUNT).astype(BF16)


def invert(parts, table, scaling):
    part = pl.BlockSpec((1, 4, 128, 8 * FC), lambda r, i: (r, i, 0, 0))
    return pl.pallas_call(
        functools.partial(invert_kernel, scaling),
        out_shape=jax.ShapeDtypeStruct((2, 8, CH, LAG_COUNT), BF16),
        grid=(2, 2),
        in_specs=[part] * (2 * CHUNKS) + [pl.BlockSpec((2 * BINS, LAG_COUNT), lambda r, i: (0, 0))],
        out_specs=pl.BlockSpec((1, 4, CH, LAG_COUNT), lambda r, i: (r, i, 0, 0)),
        compiler_params=params(),
        cost_estimate=pl.CostEstimate(
            flops=2 * 1024 * 1024 * 1024, bytes_accessed=6 << 20, transcendentals=0
        ),
        name="invert",
    )(*parts, table)


def turns(freq_ids, delay_ids):
    angles = jnp.mod(freq_ids * delay_ids, WIN_SAMPLES).astype(F32) * (2.0 * math.pi / WIN_SAMPLES)
    return jnp.cos(angles), jnp.sin(angles)


def lag_table(core):
    n = lax.broadcasted_iota(jnp.int32, (BINS, 1), 0)
    fine = n % FC
    z = (n // FC) % 8
    part = (n // (8 * FC)) % 2
    chunk = n // (16 * FC)
    freq_ids = chunk * CBINS + z * (2 * FC) + (part ^ core) * FC + fine + BAND_START
    lane = lax.broadcasted_iota(jnp.int32, (BINS, 128), 1)
    coarse = lane % 8 * 128 - LAG_COUNT // 2
    return *turns(freq_ids, lane), *turns(freq_ids, coarse)


def table_kernel(cos_a, sin_a, cos_b, sin_b, *refs):
    out = refs[-1]
    ca, sa, cb, sb = cos_a[...], sin_a[...], cos_b[...], sin_b[...]
    for n in range(LAG_COUNT // 128):
        c, s = cb[:, n : n + 1], sb[:, n : n + 1]
        out[:BINS, n * 128 : n * 128 + 128] = (ca * c - sa * s).astype(BF16)
        out[BINS:, n * 128 : n * 128 + 128] = (-(sa * c + ca * s)).astype(BF16)


def join_table(parts):
    return pl.pallas_call(
        table_kernel,
        out_shape=jax.ShapeDtypeStruct((2 * BINS, LAG_COUNT), BF16),
        in_specs=[VM] * 4,
        out_specs=VM,
        compiler_params=params(),
        cost_estimate=pl.CostEstimate(flops=8 << 20, bytes_accessed=4 << 20, transcendentals=0),
        name="table",
    )(*parts)


def device(m, z, c):
    return (m % 16) * 16 + place(z % 8) * 2 + c


EVERY = [(m, z, c) for m in range(16) for z in range(8) for c in range(2)]


def ring_back(value, r):
    pairs = [(device(m, z, c), device(m + c, z + r, c)) for m, z, c in EVERY]
    return lax.ppermute(value, ALL, pairs)


def round_ring(pieces):
    got = []
    for r in ORDER:
        got.append(ring_back(pieces[r], r))
    return got


def other_core(value):
    return lax.ppermute(value, "c", [(0, 1), (1, 0)])


def shards(spectra, valid_flags):
    z = 2 * lax.axis_index("zh") + lax.axis_index("zl")
    pos = jnp.stack([z, lax.axis_index("c")]).astype(jnp.int32)
    windows = spectra.shape[0] * lax.axis_size(("zh", "c"))
    scaling = 1.0 / math.sqrt(windows * BINS)
    flags2 = jnp.concatenate([valid_flags, valid_flags], axis=1)[:, None, :]
    *white, core = whiten(jnp.transpose(spectra, (2, 0, 1, 3)), flags2, pos)
    shift = [(device(m, z, c), device(m + 1 - 2 * c, z, c)) for m, z, c in EVERY]
    table = join_table(lag_table(core[0]))
    parts = []
    crossed, turned = (table,), ()
    for k in range(CHUNKS):
        here = lax.all_to_all(white[k], ("zl", "zh", "c"), 0, 0, tiled=True)
        there = lax.ppermute(here, ALL, shift)
        out = cross(here, there, pos, *crossed)
        crossed = (out[0],)
        same, other = turn(round_ring(out), pos, *turned)
        turned = (same,)
        parts += [same, other_core(other)]
    return invert(parts, table, scaling)


def solution(mesh):
    grid = mesh.devices.reshape(4, 4, 2, 4, 2)
    fine = Mesh(grid, ("x", "y", "zl", "zh", "c"))
    blk, seg = ("x", "y", "zl"), ("zh", "c")
    in_specs = (P(seg, blk, None, None), P(seg, blk))
    out_specs = P(None, blk + seg, None, None)


    return jax.shard_map(shards, mesh=fine, in_specs=in_specs, out_specs=out_specs, check_vma=False)
```

```python
import functools
import math

import jax
import jax.numpy as jnp
from jax import lax
from jax.experimental import pallas as pl
from jax.experimental.pallas import tpu as pltpu
from jax.sharding import Mesh, PartitionSpec as P


LAG_COUNT = 1024
WIN_SAMPLES = 15000
BAND_START = 30
SMOOTH_HALF = 32
BINS = 512
WIN = 14
CH = 64
STEP = 2
CHUNKS = 2
FC = 32 // CHUNKS
CBINS = BINS // CHUNKS
ORDER = (0, 4, 3, 5, 2, 6, 1, 7)
F32 = jnp.float32
BF16 = jnp.bfloat16

ALL = ("x", "y", "zl", "zh", "c")
VM = pl.BlockSpec(memory_space=pltpu.VMEM)
SM = pl.BlockSpec(memory_space=pltpu.SMEM)
ANY = pl.BlockSpec(memory_space=pl.ANY)


def place(z):
    return (z % 2) * 4 + z // 2


def params():
    return pltpu.CompilerParams(vmem_limit_bytes=48 << 20)


def whiten_kernel(pos_ref, spec_ref, flags_ref, *refs):
    outs, core, (band, eye, invc) = refs[:CHUNKS], refs[CHUNKS], refs[CHUNKS + 1 :]
    w = pl.program_id(0)

    @pl.when(w == 0)
    def _():
        rows = lax.broadcasted_iota(jnp.int32, (BINS, BINS), 0)
        cols = lax.broadcasted_iota(jnp.int32, (BINS, BINS), 1)
        band[...] = jnp.where(jnp.abs(rows - cols) <= SMOOTH_HALF, 1.0, 0.0).astype(BF16)
        r2 = lax.broadcasted_iota(jnp.int32, (256, 256), 0)
        c2 = lax.broadcasted_iota(jnp.int32, (256, 256), 1)
        eye[...] = jnp.where(r2 == c2, 1.0, 0.0).astype(BF16)
        f = lax.broadcasted_iota(jnp.int32, (BINS, 128), 0)
        count = jnp.minimum(f + SMOOTH_HALF, BINS - 1) - jnp.maximum(f - SMOOTH_HALF, 0) + 1
        invc[...] = 1.0 / count.astype(F32)

    nt = (((1,), (1,)), ((), ()))
    for v in range(STEP):
        re16, im16 = spec_ref[0, v], spec_ref[1, v]
        re, im = re16.astype(F32), im16.astype(F32)
        amp = jnp.sqrt(re * re + im * im).astype(BF16)
        amp2 = jnp.concatenate([amp, amp], axis=0)
        both = jnp.concatenate([re16, im16], axis=0)
        summed = lax.dot_general(band[...], amp2, nt, preferred_element_type=F32)
        scale = flags_ref[v].astype(F32) / (summed * invc[...] + 1e-05)
        for h in range(2):
            half = lax.dot_general(
                eye[...], both[:, h * 256 : (h + 1) * 256], nt, preferred_element_type=F32
            )
            white = (half * scale[h * 256 : (h + 1) * 256]).astype(BF16)
            for n in range(256 // FC):
                k, d = divmod(h * 256 // FC + n, 16)
                outs[k][place(d // 2) * 2 + d % 2, w * STEP + v] = white[n * FC : (n + 1) * FC]
    core[0] = pos_ref[1]


def whiten(spec, flags2, pos):
    shape = pltpu.HBM((16, WIN, FC, 128), BF16)
    full = pl.BlockSpec((16, WIN, FC, 128), lambda w, *_: (0, 0, 0, 0))
    return pl.pallas_call(
        whiten_kernel,
        out_shape=[shape] * CHUNKS + [jax.ShapeDtypeStruct((1,), jnp.int32)],
        grid_spec=pltpu.PrefetchScalarGridSpec(
            num_scalar_prefetch=1,
            grid=(WIN // STEP,),
            in_specs=[
                pl.BlockSpec((2, STEP, CH, BINS), lambda w, *_: (0, w, 0, 0)),
                pl.BlockSpec((STEP, 1, 128), lambda w, *_: (w, 0, 0)),
            ],
            out_specs=[full] * CHUNKS + [SM],
            scratch_shapes=[
                pltpu.VMEM((BINS, BINS), BF16),
                pltpu.VMEM((256, 256), BF16),
                pltpu.VMEM((BINS, 128), F32),
            ],
        ),
        compiler_params=params(),
        cost_estimate=pl.CostEstimate(
            flops=3 * 512 * 512 * 128 * WIN, bytes_accessed=4 << 20, transcendentals=0
        ),
        name="whiten",
    )(pos, spec, flags2)


def cross_kernel(turned, pos_ref, here, there, *refs):
    outs, (wide, res) = refs[-10:-2], refs[-2:]
    z, c = pos_ref[0], pos_ref[1]
    rows = 8 * WIN * FC
    for n, ref in enumerate((here, there)):
        for b in range(2):
            base = pl.multiple_of(((n ^ c if turned else n) * 2 + b) * rows, rows)
            wide[pl.ds(base, rows)] = ref[8 * b : 8 * b + 8].reshape(rows, 128).astype(F32)
    sign = jnp.where(lax.broadcasted_iota(jnp.int32, (CH, 128), 1) < CH, 1.0, -1.0).astype(F32)
    tn = (((0,), (0,)), ((), ()))

    def one_bin(f, carry):
        x = [
            wide[pl.ds(n * rows + f, 8 * WIN, stride=FC), :].astype(BF16) for n in range(4)
        ]
        own_a, own_b, prev_a, prev_b = x
        for b, (left, rights) in enumerate(
            ((own_a, (prev_b, prev_a)), (own_b, (own_a, prev_b)))
        ):
            g = lax.dot_general(
                left, jnp.concatenate(rights, axis=1), tn, preferred_element_type=F32
            )
            for rnd in range(2):
                top = g[:CH, rnd * 128 : rnd * 128 + 128]
                bottom = pltpu.roll(g[CH:, rnd * 128 : rnd * 128 + 128], CH, 1)
                start = pl.multiple_of(((rnd * 2 + b) * FC + f) * CH, CH)
                res[pl.ds(start, CH), :] = bottom + sign * top
        return carry

    lax.fori_loop(0, FC, one_bin, 0, unroll=2)
    for r in range(8):
        dst = (z + r) & 7
        for crel in range(2):
            row = ((dst >> 1) * 2 + (c ^ crel)) * 8
            for rnd in range(2):
                base = (rnd * 2 + (dst & 1)) * FC * CH + row
                for i in range(8):
                    outs[r][crel, rnd, i] = res[pl.ds(base + i, FC, stride=CH), :].astype(BF16)


def cross(turned, here, there, pos, *after):
    shape = jax.ShapeDtypeStruct((2, 2, 8, FC, 128), BF16)
    return pl.pallas_call(
        functools.partial(cross_kernel, turned),
        out_shape=[shape] * 8,
        in_specs=[SM] + [VM] * 2 + [ANY] * len(after),
        out_specs=[VM] * 8,
        scratch_shapes=[
            pltpu.VMEM((32 * WIN * FC, 128), F32),
            pltpu.VMEM((4 * FC * CH, 128), F32),
        ],
        compiler_params=params(),
        cost_estimate=pl.CostEstimate(
            flops=4 * FC * 128 * 256 * 256, bytes_accessed=3 << 20, transcendentals=0
        ),
        name="cross",
    )(pos, here, there, *after)


def turn_kernel(pos_ref, *refs):
    ins, (same, other, buf) = refs[:8], refs[-3:]
    z = pos_ref[0]
    for crel, out in enumerate((same, other)):
        for rnd in range(2):
            for i in range(8):
                for n, r in enumerate(ORDER):
                    start = pl.multiple_of(((z - r) & 7) * FC, FC)
                    buf[pl.ds(start, FC), :] = ins[n][crel, rnd, i].astype(F32)
                out[rnd, i] = buf[...].T.astype(BF16)


def turn(pieces, pos, *after):
    shape = jax.ShapeDtypeStruct((2, 8, 128, 8 * FC), BF16)
    return pl.pallas_call(
        turn_kernel,
        out_shape=[shape] * 2,
        in_specs=[SM] + [VM] * 8 + [ANY] * len(after),
        out_specs=[VM] * 2,
        scratch_shapes=[pltpu.VMEM((8 * FC, 128), F32)],
        compiler_params=params(),
        cost_estimate=pl.CostEstimate(flops=0, bytes_accessed=4 << 20, transcendentals=0),
        name="turn",
    )(pos, *pieces, *after)


def invert_kernel(scaling, *refs):
    parts, (table, out) = refs[: 2 * CHUNKS], refs[2 * CHUNKS :]
    rows = []
    for i in range(4):
        cols = [p[0, i, k * CH : (k + 1) * CH] for k in range(2) for p in parts]
        rows.append(jnp.concatenate(cols, axis=1))
    left = jnp.concatenate(rows, axis=0)
    result = jnp.dot(left, table[...], preferred_element_type=F32) * scaling
    out[0] = result.reshape(4, CH, LAG_COUNT).astype(BF16)


def invert(parts, table, scaling):
    part = pl.BlockSpec((1, 4, 128, 8 * FC), lambda r, i: (r, i, 0, 0))
    return pl.pallas_call(
        functools.partial(invert_kernel, scaling),
        out_shape=jax.ShapeDtypeStruct((2, 8, CH, LAG_COUNT), BF16),
        grid=(2, 2),
        in_specs=[part] * (2 * CHUNKS) + [pl.BlockSpec((2 * BINS, LAG_COUNT), lambda r, i: (0, 0))],
        out_specs=pl.BlockSpec((1, 4, CH, LAG_COUNT), lambda r, i: (r, i, 0, 0)),
        compiler_params=params(),
        cost_estimate=pl.CostEstimate(
            flops=2 * 1024 * 1024 * 1024, bytes_accessed=6 << 20, transcendentals=0
        ),
        name="invert",
    )(*parts, table)


def turns(freq_ids, delay_ids):
    angles = jnp.mod(freq_ids * delay_ids, WIN_SAMPLES).astype(F32) * (2.0 * math.pi / WIN_SAMPLES)
    return jnp.cos(angles), jnp.sin(angles)


def lag_table(core):
    n = lax.broadcasted_iota(jnp.int32, (BINS, 1), 0)
    fine = n % FC
    z = (n // FC) % 8
    part = (n // (8 * FC)) % 2
    chunk = n // (16 * FC)
    freq_ids = chunk * CBINS + z * (2 * FC) + (part ^ core) * FC + fine + BAND_START
    lane = lax.broadcasted_iota(jnp.int32, (BINS, 128), 1)
    coarse = lane % 8 * 128 - LAG_COUNT // 2
    return *turns(freq_ids, lane), *turns(freq_ids, coarse)


def table_kernel(cos_a, sin_a, cos_b, sin_b, *refs):
    out = refs[-1]
    ca, sa, cb, sb = cos_a[...], sin_a[...], cos_b[...], sin_b[...]
    for n in range(LAG_COUNT // 128):
        c, s = cb[:, n : n + 1], sb[:, n : n + 1]
        out[:BINS, n * 128 : n * 128 + 128] = (ca * c - sa * s).astype(BF16)
        out[BINS:, n * 128 : n * 128 + 128] = (-(sa * c + ca * s)).astype(BF16)


def join_table(parts):
    return pl.pallas_call(
        table_kernel,
        out_shape=jax.ShapeDtypeStruct((2 * BINS, LAG_COUNT), BF16),
        in_specs=[VM] * 4,
        out_specs=VM,
        compiler_params=params(),
        cost_estimate=pl.CostEstimate(flops=8 << 20, bytes_accessed=4 << 20, transcendentals=0),
        name="table",
    )(*parts)


def device(m, z, c):
    return (m % 16) * 16 + place(z % 8) * 2 + c


EVERY = [(m, z, c) for m in range(16) for z in range(8) for c in range(2)]


def round_ring(pieces, turned):
    got = []
    for r in ORDER:
        pairs = [(device(m, z, c), device(m + c * turned, z + r, c)) for m, z, c in EVERY]
        got.append(lax.ppermute(pieces[r], ALL, pairs) if r or turned else pieces[r])
    return got


def other_core(value):
    return lax.ppermute(value, "c", [(0, 1), (1, 0)])


def shards(spectra, valid_flags):
    z = 2 * lax.axis_index("zh") + lax.axis_index("zl")
    pos = jnp.stack([z, lax.axis_index("c")]).astype(jnp.int32)
    windows = spectra.shape[0] * lax.axis_size(("zh", "c"))
    scaling = 1.0 / math.sqrt(windows * BINS)
    flags2 = jnp.concatenate([valid_flags, valid_flags], axis=1)[:, None, :]
    *white, core = whiten(jnp.transpose(spectra, (2, 0, 1, 3)), flags2, pos)
    table = join_table(lag_table(core[0]))
    parts = []
    crossed, turned = (table,), ()
    for k in range(CHUNKS):
        turned_round = int(k == CHUNKS - 1)
        shift = [
            (device(m, z, c), device(m + 1 - 2 * c * turned_round, z, c)) for m, z, c in EVERY
        ]
        here = lax.all_to_all(white[k], ("zl", "zh", "c"), 0, 0, tiled=True)
        there = lax.ppermute(here, ALL, shift)
        out = cross(turned_round, here, there, pos, *crossed)
        crossed = (out[0],)
        same, other = turn(round_ring(out, turned_round), pos, *turned)
        turned = (same,)
        parts += [same, other_core(other)]
    return invert(parts, table, scaling)


def solution(mesh):
    grid = mesh.devices.reshape(4, 4, 2, 4, 2)
    fine = Mesh(grid, ("x", "y", "zl", "zh", "c"))
    blk, seg = ("x", "y", "zl"), ("zh", "c")
    in_specs = (P(seg, blk, None, None), P(seg, blk))
    out_specs = P(None, blk + seg, None, None)


    return jax.shard_map(shards, mesh=fine, in_specs=in_specs, out_specs=out_specs, check_vma=False)
```

```python
import functools
import math

import jax
import jax.numpy as jnp
from jax import lax
from jax.experimental import pallas as pl
from jax.experimental.pallas import tpu as pltpu
from jax.sharding import Mesh, PartitionSpec as P


LAG_COUNT = 1024
WIN_SAMPLES = 15000
BAND_START = 30
SMOOTH_HALF = 32
BINS = 512
WIN = 14
CH = 64
STEP = 2
CHUNKS = 2
FC = 32 // CHUNKS
CBINS = BINS // CHUNKS
ORDER = (0, 4, 3, 5, 2, 6, 1, 7)
F32 = jnp.float32
BF16 = jnp.bfloat16

ALL = ("x", "y", "zl", "zh", "c")
VM = pl.BlockSpec(memory_space=pltpu.VMEM)
SM = pl.BlockSpec(memory_space=pltpu.SMEM)
ANY = pl.BlockSpec(memory_space=pl.ANY)


def params():
    return pltpu.CompilerParams(vmem_limit_bytes=24 << 20)


def whiten_kernel(pos_ref, spec_ref, flags_ref, *refs):
    outs, core = refs[: 8 * CHUNKS], refs[8 * CHUNKS]
    band, eye, invc, white = refs[8 * CHUNKS + 1 :]
    w = pl.program_id(0)
    z, c = pos_ref[0], pos_ref[1]

    @pl.when(w == 0)
    def _():
        rows = lax.broadcasted_iota(jnp.int32, (BINS, BINS), 0)
        cols = lax.broadcasted_iota(jnp.int32, (BINS, BINS), 1)
        band[...] = jnp.where(jnp.abs(rows - cols) <= SMOOTH_HALF, 1.0, 0.0).astype(BF16)
        r2 = lax.broadcasted_iota(jnp.int32, (256, 256), 0)
        c2 = lax.broadcasted_iota(jnp.int32, (256, 256), 1)
        eye[...] = jnp.where(r2 == c2, 1.0, 0.0).astype(BF16)
        f = lax.broadcasted_iota(jnp.int32, (BINS, 128), 0)
        count = jnp.minimum(f + SMOOTH_HALF, BINS - 1) - jnp.maximum(f - SMOOTH_HALF, 0) + 1
        invc[...] = 1.0 / count.astype(F32)

    nt = (((1,), (1,)), ((), ()))
    for v in range(STEP):
        re16, im16 = spec_ref[0, v], spec_ref[1, v]
        re, im = re16.astype(F32), im16.astype(F32)
        amp = jnp.sqrt(re * re + im * im).astype(BF16)
        amp2 = jnp.concatenate([amp, amp], axis=0)
        both = jnp.concatenate([re16, im16], axis=0)
        summed = lax.dot_general(band[...], amp2, nt, preferred_element_type=F32)
        scale = flags_ref[v].astype(F32) / (summed * invc[...] + 1e-05)
        for h in range(2):
            half = lax.dot_general(
                eye[...], both[:, h * 256 : (h + 1) * 256], nt, preferred_element_type=F32
            )
            part = half * scale[h * 256 : (h + 1) * 256]
            white[v, h * 256 : (h + 1) * 256] = part.astype(BF16)
    for k in range(CHUNKS):
        for r in range(8):
            base = k * CBINS + ((z + r) & 7) * (2 * FC)
            for crel in range(2):
                start = pl.multiple_of(base + (c ^ crel) * FC, FC)
                for v in range(STEP):
                    outs[k * 8 + r][crel, w * STEP + v] = white[v, pl.ds(start, FC), :]
    core[0] = c


def whiten(spec, flags2, pos):
    shape = jax.ShapeDtypeStruct((2, WIN, FC, 128), BF16)
    full = pl.BlockSpec((2, WIN, FC, 128), lambda w, *_: (0, 0, 0, 0))
    return pl.pallas_call(
        whiten_kernel,
        out_shape=[shape] * (8 * CHUNKS) + [jax.ShapeDtypeStruct((1,), jnp.int32)],
        grid_spec=pltpu.PrefetchScalarGridSpec(
            num_scalar_prefetch=1,
            grid=(WIN // STEP,),
            in_specs=[
                pl.BlockSpec((2, STEP, CH, BINS), lambda w, *_: (0, w, 0, 0)),
                pl.BlockSpec((STEP, 1, 128), lambda w, *_: (w, 0, 0)),
            ],
            out_specs=[full] * (8 * CHUNKS) + [SM],
            scratch_shapes=[
                pltpu.VMEM((BINS, BINS), BF16),
                pltpu.VMEM((256, 256), BF16),
                pltpu.VMEM((BINS, 128), F32),
                pltpu.VMEM((STEP, BINS, 128), BF16),
            ],
        ),
        compiler_params=params(),
        cost_estimate=pl.CostEstimate(
            flops=3 * 512 * 512 * 128 * WIN, bytes_accessed=4 << 20, transcendentals=0
        ),
        name="whiten",
    )(pos, spec, flags2)


def merge_kernel(pos_ref, *refs):
    ins, (same, other) = refs[:8], refs[-2:]
    z = pos_ref[0]
    for n, r in enumerate(ORDER):
        src = (z - r) & 7
        same[src & 1, src >> 1] = ins[n][0]
        other[src & 1, src >> 1] = ins[n][1]


def merge(pieces, pos, *after):
    shape = jax.ShapeDtypeStruct((2, 4, WIN, FC, 128), BF16)
    return pl.pallas_call(
        merge_kernel,
        out_shape=[shape] * 2,
        in_specs=[SM] + [VM] * 8 + [ANY] * len(after),
        out_specs=[VM] * 2,
        compiler_params=params(),
        cost_estimate=pl.CostEstimate(
            flops=0, bytes_accessed=4 * 8 * WIN * FC * 256, transcendentals=0
        ),
        name="merge",
    )(pos, *pieces, *after)


def cross_kernel(turned, pos_ref, own0, own1, prev0, prev1, *refs):
    outs, (wide, res) = refs[-10:-2], refs[-2:]
    z, c = pos_ref[0], pos_ref[1]
    rows = 4 * WIN * FC
    for n, (first, second) in enumerate(((own0, own1), (prev0, prev1))):
        for b in range(2):
            base = pl.multiple_of(((n ^ c if turned else n) * 2 + b) * 2 * rows, rows)
            wide[pl.ds(base, rows)] = first[b].reshape(rows, 128).astype(F32)
            wide[pl.ds(base + rows, rows)] = second[b].reshape(rows, 128).astype(F32)
    sign = jnp.where(lax.broadcasted_iota(jnp.int32, (CH, 128), 1) < CH, 1.0, -1.0).astype(F32)
    tn = (((0,), (0,)), ((), ()))

    def one_bin(f, carry):
        x = [
            wide[pl.ds(n * 2 * rows + f, 8 * WIN, stride=FC), :].astype(BF16) for n in range(4)
        ]
        own_a, own_b, prev_a, prev_b = x
        for b, (left, rights) in enumerate(
            ((own_a, (prev_b, prev_a)), (own_b, (own_a, prev_b)))
        ):
            g = lax.dot_general(
                left, jnp.concatenate(rights, axis=1), tn, preferred_element_type=F32
            )
            for rnd in range(2):
                top = g[:CH, rnd * 128 : rnd * 128 + 128]
                bottom = pltpu.roll(g[CH:, rnd * 128 : rnd * 128 + 128], CH, 1)
                start = pl.multiple_of(((rnd * 2 + b) * FC + f) * CH, CH)
                res[pl.ds(start, CH), :] = bottom + sign * top
        return carry

    lax.fori_loop(0, FC, one_bin, 0, unroll=2)
    for r in range(8):
        dst = (z + r) & 7
        for crel in range(2):
            row = ((dst >> 1) * 2 + (c ^ crel)) * 8
            for rnd in range(2):
                base = (rnd * 2 + (dst & 1)) * FC * CH + row
                for i in range(8):
                    outs[r][crel, rnd, i] = res[pl.ds(base + i, FC, stride=CH), :].astype(BF16)


def cross(turned, own0, own1, prev0, prev1, pos, *after):
    shape = jax.ShapeDtypeStruct((2, 2, 8, FC, 128), BF16)
    return pl.pallas_call(
        functools.partial(cross_kernel, turned),
        out_shape=[shape] * 8,
        in_specs=[SM] + [VM] * 4 + [ANY] * len(after),
        out_specs=[VM] * 8,
        scratch_shapes=[
            pltpu.VMEM((32 * WIN * FC, 128), F32),
            pltpu.VMEM((4 * FC * CH, 128), F32),
        ],
        compiler_params=params(),
        cost_estimate=pl.CostEstimate(
            flops=4 * FC * 128 * 256 * 256, bytes_accessed=3 << 20, transcendentals=0
        ),
        name="cross",
    )(pos, own0, own1, prev0, prev1, *after)


def turn_kernel(pos_ref, *refs):
    ins, (same, other, buf) = refs[:8], refs[-3:]
    z = pos_ref[0]
    for crel, out in enumerate((same, other)):
        for rnd in range(2):
            for i in range(8):
                for n, r in enumerate(ORDER):
                    start = pl.multiple_of(((z - r) & 7) * FC, FC)
                    buf[pl.ds(start, FC), :] = ins[n][crel, rnd, i].astype(F32)
                out[rnd, i] = buf[...].T.astype(BF16)


def turn(pieces, pos, *after):
    shape = jax.ShapeDtypeStruct((2, 8, 128, 8 * FC), BF16)
    return pl.pallas_call(
        turn_kernel,
        out_shape=[shape] * 2,
        in_specs=[SM] + [VM] * 8 + [ANY] * len(after),
        out_specs=[VM] * 2,
        scratch_shapes=[pltpu.VMEM((8 * FC, 128), F32)],
        compiler_params=params(),
        cost_estimate=pl.CostEstimate(flops=0, bytes_accessed=4 << 20, transcendentals=0),
        name="turn",
    )(pos, *pieces, *after)


def invert_kernel(scaling, *refs):
    parts, (table, out) = refs[: 2 * CHUNKS], refs[2 * CHUNKS :]
    rows = []
    for i in range(4):
        cols = [p[0, i, k * CH : (k + 1) * CH] for k in range(2) for p in parts]
        rows.append(jnp.concatenate(cols, axis=1))
    left = jnp.concatenate(rows, axis=0)
    result = jnp.dot(left, table[...], preferred_element_type=F32) * scaling
    out[0] = result.reshape(4, CH, LAG_COUNT).astype(BF16)


def invert(parts, table, scaling):
    part = pl.BlockSpec((1, 4, 128, 8 * FC), lambda r, i: (r, i, 0, 0))
    return pl.pallas_call(
        functools.partial(invert_kernel, scaling),
        out_shape=jax.ShapeDtypeStruct((2, 8, CH, LAG_COUNT), BF16),
        grid=(2, 2),
        in_specs=[part] * (2 * CHUNKS) + [pl.BlockSpec((2 * BINS, LAG_COUNT), lambda r, i: (0, 0))],
        out_specs=pl.BlockSpec((1, 4, CH, LAG_COUNT), lambda r, i: (r, i, 0, 0)),
        compiler_params=params(),
        cost_estimate=pl.CostEstimate(
            flops=2 * 1024 * 1024 * 1024, bytes_accessed=6 << 20, transcendentals=0
        ),
        name="invert",
    )(*parts, table)


def turns(freq_ids, delay_ids):
    angles = jnp.mod(freq_ids * delay_ids, WIN_SAMPLES).astype(F32) * (2.0 * math.pi / WIN_SAMPLES)
    return jnp.cos(angles), jnp.sin(angles)


def lag_table(core):
    n = lax.broadcasted_iota(jnp.int32, (BINS, 1), 0)
    fine = n % FC
    z = (n // FC) % 8
    part = (n // (8 * FC)) % 2
    chunk = n // (16 * FC)
    freq_ids = chunk * CBINS + z * (2 * FC) + (part ^ core) * FC + fine + BAND_START
    lane = lax.broadcasted_iota(jnp.int32, (BINS, 128), 1)
    coarse = lane % 8 * 128 - LAG_COUNT // 2
    return *turns(freq_ids, lane), *turns(freq_ids, coarse)


def table_kernel(cos_a, sin_a, cos_b, sin_b, *refs):
    out = refs[-1]
    ca, sa, cb, sb = cos_a[...], sin_a[...], cos_b[...], sin_b[...]
    for n in range(LAG_COUNT // 128):
        c, s = cb[:, n : n + 1], sb[:, n : n + 1]
        out[:BINS, n * 128 : n * 128 + 128] = (ca * c - sa * s).astype(BF16)
        out[BINS:, n * 128 : n * 128 + 128] = (-(sa * c + ca * s)).astype(BF16)


def join_table(parts):
    return pl.pallas_call(
        table_kernel,
        out_shape=jax.ShapeDtypeStruct((2 * BINS, LAG_COUNT), BF16),
        in_specs=[VM] * 4,
        out_specs=VM,
        compiler_params=params(),
        cost_estimate=pl.CostEstimate(flops=8 << 20, bytes_accessed=4 << 20, transcendentals=0),
        name="table",
    )(*parts)


def place(z):
    return (z % 2) * 4 + z // 2


def device(m, z, c):
    return (m % 16) * 16 + place(z % 8) * 2 + c


EVERY = [(m, z, c) for m in range(16) for z in range(8) for c in range(2)]


def send(value, target):
    return lax.ppermute(value, ALL, [(device(*d), device(*target(*d))) for d in EVERY])


def round_ring(pieces, turned=0):
    got = []
    for r in ORDER:
        if r or turned:
            got.append(send(pieces[r], lambda m, z, c: (m + c * turned, z + r, c)))
        else:
            got.append(pieces[r])
    return got


def other_core(value):
    return send(value, lambda m, z, c: (m, z, 1 - c))


def shards(spectra, valid_flags):
    z = 2 * lax.axis_index("zh") + lax.axis_index("zl")
    pos = jnp.stack([z, lax.axis_index("c")]).astype(jnp.int32)
    windows = spectra.shape[0] * lax.axis_size(("zh", "c"))
    scaling = 1.0 / math.sqrt(windows * BINS)
    flags2 = jnp.concatenate([valid_flags, valid_flags], axis=1)[:, None, :]
    *white, core = whiten(jnp.transpose(spectra, (2, 0, 1, 3)), flags2, pos)
    table = join_table(lag_table(core[0]))
    parts = []
    merged, crossed, turned = (table,), (), ()
    for k in range(CHUNKS):
        back = int(k == CHUNKS - 1)
        got = round_ring(white[k * 8 : k * 8 + 8])
        same, other = merge(got, pos, *merged)
        merged = (same,)
        prev0 = send(same, lambda m, z, c: (m + 1 - 2 * c * back, z, c))
        prev1 = send(other, lambda m, z, c: (m + 1 - 2 * (1 - c) * back, z, 1 - c))
        own1 = other_core(other)
        out = cross(back, same, own1, prev0, prev1, pos, *crossed)
        crossed = (out[0],)
        same, other = turn(round_ring(out, back), pos, *turned)
        turned = (same,)
        parts += [same, other_core(other)]
    return invert(parts, table, scaling)


def solution(mesh):
    grid = mesh.devices.reshape(4, 4, 2, 4, 2)
    fine = Mesh(grid, ("x", "y", "zl", "zh", "c"))
    blk, seg = ("x", "y", "zl"), ("zh", "c")
    in_specs = (P(seg, blk, None, None), P(seg, blk))
    out_specs = P(None, blk + seg, None, None)


    return jax.shard_map(shards, mesh=fine, in_specs=in_specs, out_specs=out_specs, check_vma=False)
```

```python
import functools
import math

import jax
import jax.numpy as jnp
from jax import lax
from jax.experimental import pallas as pl
from jax.experimental.pallas import tpu as pltpu
from jax.sharding import Mesh, PartitionSpec as P


LAG_COUNT = 1024
WIN_SAMPLES = 15000
BAND_START = 30
SMOOTH_HALF = 32
BINS = 512
WIN = 14
CH = 64
STEP = 2
CHUNKS = 2
FC = 32 // CHUNKS
CBINS = BINS // CHUNKS
ORDER = (0, 4, 3, 5, 2, 6, 1, 7)
F32 = jnp.float32
BF16 = jnp.bfloat16

ALL = ("x", "y", "zl", "zh", "c")
VM = pl.BlockSpec(memory_space=pltpu.VMEM)
SM = pl.BlockSpec(memory_space=pltpu.SMEM)
ANY = pl.BlockSpec(memory_space=pl.ANY)


def params():
    return pltpu.CompilerParams(vmem_limit_bytes=24 << 20)


def whiten_kernel(pos_ref, spec_ref, flags_ref, *refs):
    outs, core = refs[: 8 * CHUNKS], refs[8 * CHUNKS]
    band, eye, invc, white = refs[8 * CHUNKS + 1 :]
    w = pl.program_id(0)
    z, c = pos_ref[0], pos_ref[1]

    @pl.when(w == 0)
    def _():
        rows = lax.broadcasted_iota(jnp.int32, (BINS, BINS), 0)
        cols = lax.broadcasted_iota(jnp.int32, (BINS, BINS), 1)
        band[...] = jnp.where(jnp.abs(rows - cols) <= SMOOTH_HALF, 1.0, 0.0).astype(BF16)
        r2 = lax.broadcasted_iota(jnp.int32, (256, 256), 0)
        c2 = lax.broadcasted_iota(jnp.int32, (256, 256), 1)
        eye[...] = jnp.where(r2 == c2, 1.0, 0.0).astype(BF16)
        f = lax.broadcasted_iota(jnp.int32, (BINS, 128), 0)
        count = jnp.minimum(f + SMOOTH_HALF, BINS - 1) - jnp.maximum(f - SMOOTH_HALF, 0) + 1
        invc[...] = 1.0 / count.astype(F32)

    nt = (((1,), (1,)), ((), ()))
    for v in range(STEP):
        re16, im16 = spec_ref[0, v], spec_ref[1, v]
        re, im = re16.astype(F32), im16.astype(F32)
        amp = jnp.sqrt(re * re + im * im).astype(BF16)
        amp2 = jnp.concatenate([amp, amp], axis=0)
        both = jnp.concatenate([re16, im16], axis=0)
        summed = lax.dot_general(band[...], amp2, nt, preferred_element_type=F32)
        scale = flags_ref[v].astype(F32) / (summed * invc[...] + 1e-05)
        for h in range(2):
            half = lax.dot_general(
                eye[...], both[:, h * 256 : (h + 1) * 256], nt, preferred_element_type=F32
            )
            part = half * scale[h * 256 : (h + 1) * 256]
            white[v, h * 256 : (h + 1) * 256] = part.astype(BF16)
    for k in range(CHUNKS):
        for r in range(8):
            base = k * CBINS + ((z + r) & 7) * (2 * FC)
            for crel in range(2):
                start = pl.multiple_of(base + (c ^ crel) * FC, FC)
                for v in range(STEP):
                    outs[k * 8 + r][crel, w * STEP + v] = white[v, pl.ds(start, FC), :]
    core[0] = c


def whiten(spec, flags2, pos):
    shape = jax.ShapeDtypeStruct((2, WIN, FC, 128), BF16)
    full = pl.BlockSpec((2, WIN, FC, 128), lambda w, *_: (0, 0, 0, 0))
    return pl.pallas_call(
        whiten_kernel,
        out_shape=[shape] * (8 * CHUNKS) + [jax.ShapeDtypeStruct((1,), jnp.int32)],
        grid_spec=pltpu.PrefetchScalarGridSpec(
            num_scalar_prefetch=1,
            grid=(WIN // STEP,),
            in_specs=[
                pl.BlockSpec((2, STEP, CH, BINS), lambda w, *_: (0, w, 0, 0)),
                pl.BlockSpec((STEP, 1, 128), lambda w, *_: (w, 0, 0)),
            ],
            out_specs=[full] * (8 * CHUNKS) + [SM],
            scratch_shapes=[
                pltpu.VMEM((BINS, BINS), BF16),
                pltpu.VMEM((256, 256), BF16),
                pltpu.VMEM((BINS, 128), F32),
                pltpu.VMEM((STEP, BINS, 128), BF16),
            ],
        ),
        compiler_params=params(),
        cost_estimate=pl.CostEstimate(
            flops=3 * 512 * 512 * 128 * WIN, bytes_accessed=4 << 20, transcendentals=0
        ),
        name="whiten",
    )(pos, spec, flags2)


def merge_kernel(pos_ref, *refs):
    ins, (same, other) = refs[:8], refs[-2:]
    z = pos_ref[0]
    for n, r in enumerate(ORDER):
        src = (z - r) & 7
        same[src & 1, src >> 1] = ins[n][0]
        other[src & 1, src >> 1] = ins[n][1]


def merge(pieces, pos, *after):
    shape = jax.ShapeDtypeStruct((2, 4, WIN, FC, 128), BF16)
    return pl.pallas_call(
        merge_kernel,
        out_shape=[shape] * 2,
        in_specs=[SM] + [VM] * 8 + [ANY] * len(after),
        out_specs=[VM] * 2,
        compiler_params=params(),
        cost_estimate=pl.CostEstimate(
            flops=0, bytes_accessed=4 * 8 * WIN * FC * 256, transcendentals=0
        ),
        name="merge",
    )(pos, *pieces, *after)


def cross_kernel(pos_ref, own0, own1, prev0, prev1, *refs):
    outs, (wide, res) = refs[-10:-2], refs[-2:]
    z, c = pos_ref[0], pos_ref[1]
    rows = 4 * WIN * FC
    for n, (first, second) in enumerate(((own0, own1), (prev0, prev1))):
        for b in range(2):
            base = pl.multiple_of(((n ^ c) * 2 + b) * 2 * rows, rows)
            wide[pl.ds(base, rows)] = first[b].reshape(rows, 128).astype(F32)
            wide[pl.ds(base + rows, rows)] = second[b].reshape(rows, 128).astype(F32)
    sign = jnp.where(lax.broadcasted_iota(jnp.int32, (CH, 128), 1) < CH, 1.0, -1.0).astype(F32)
    tn = (((0,), (0,)), ((), ()))

    def one_bin(f, carry):
        x = [
            wide[pl.ds(n * 2 * rows + f, 8 * WIN, stride=FC), :].astype(BF16) for n in range(4)
        ]
        own_a, own_b, prev_a, prev_b = x
        for b, (left, rights) in enumerate(
            ((own_a, (prev_b, prev_a)), (own_b, (own_a, prev_b)))
        ):
            g = lax.dot_general(
                left, jnp.concatenate(rights, axis=1), tn, preferred_element_type=F32
            )
            for rnd in range(2):
                top = g[:CH, rnd * 128 : rnd * 128 + 128]
                bottom = pltpu.roll(g[CH:, rnd * 128 : rnd * 128 + 128], CH, 1)
                start = pl.multiple_of(((rnd * 2 + b) * FC + f) * CH, CH)
                res[pl.ds(start, CH), :] = bottom + sign * top
        return carry

    lax.fori_loop(0, FC, one_bin, 0, unroll=2)
    for r in range(8):
        dst = (z + r) & 7
        for crel in range(2):
            row = ((dst >> 1) * 2 + (c ^ crel)) * 8
            for rnd in range(2):
                base = (rnd * 2 + (dst & 1)) * FC * CH + row

                @pl.loop(0, 8, unroll=2)
                def _(i, r=r, crel=crel, rnd=rnd, base=base):
                    outs[r][crel, rnd, i] = res[pl.ds(base + i, FC, stride=CH), :].astype(BF16)


def cross(own0, own1, prev0, prev1, pos, *after):
    shape = jax.ShapeDtypeStruct((2, 2, 8, FC, 128), BF16)
    return pl.pallas_call(
        cross_kernel,
        out_shape=[shape] * 8,
        in_specs=[SM] + [VM] * 4 + [ANY] * len(after),
        out_specs=[VM] * 8,
        scratch_shapes=[
            pltpu.VMEM((32 * WIN * FC, 128), F32),
            pltpu.VMEM((4 * FC * CH, 128), F32),
        ],
        compiler_params=params(),
        cost_estimate=pl.CostEstimate(
            flops=4 * FC * 128 * 256 * 256, bytes_accessed=3 << 20, transcendentals=0
        ),
        name="cross",
    )(pos, own0, own1, prev0, prev1, *after)


def turn_kernel(pos_ref, *refs):
    ins, (out, buf) = refs[:8], refs[-2:]
    z = pos_ref[0]
    for rnd in range(2):

        @pl.loop(0, 8, unroll=2)
        def _(i, rnd=rnd):
            slot = i & 1
            for n, r in enumerate(ORDER):
                start = pl.multiple_of(((z - r) & 7) * FC, FC)
                buf[slot, pl.ds(start, FC), :] = ins[n][0, rnd, i].astype(F32)
            out[rnd, i] = buf[slot].T.astype(BF16)


def turn(crel, pieces, pos, *after):
    half = pl.BlockSpec((1, 2, 8, FC, 128), lambda n: (crel, 0, 0, 0, 0))
    whole = pl.BlockSpec((2, 8, 128, 8 * FC), lambda n: (0, 0, 0, 0))
    return pl.pallas_call(
        turn_kernel,
        out_shape=jax.ShapeDtypeStruct((2, 8, 128, 8 * FC), BF16),
        grid=(1,),
        in_specs=[SM] + [half] * 8 + [ANY] * len(after),
        out_specs=whole,
        scratch_shapes=[pltpu.VMEM((2, 8 * FC, 128), F32)],
        compiler_params=params(),
        cost_estimate=pl.CostEstimate(flops=0, bytes_accessed=2 << 20, transcendentals=0),
        name="turn",
    )(pos, *pieces, *after)


def invert_kernel(scaling, chunk, *refs):
    parts, table, sums, out = refs[:2], refs[2], refs[3:-1], refs[-1]
    total = 0.0
    for k in range(2):
        rows = []
        for i in range(4):
            cols = [p[0, i, k * CH : (k + 1) * CH] for p in parts]
            rows.append(jnp.concatenate(cols, axis=1))
        start = k * BINS + chunk * CBINS
        total += jnp.dot(
            jnp.concatenate(rows, axis=0),
            table[start : start + CBINS],
            preferred_element_type=F32,
        )
    total = total.reshape(4, CH, LAG_COUNT)
    for ref in sums:
        total += ref[0]
    if chunk == CHUNKS - 1:
        total = total * scaling
    out[0] = total.astype(out.dtype)


def invert(chunk, parts, table, sums, scaling):
    part = pl.BlockSpec((1, 4, 128, 8 * FC), lambda r, i: (r, i, 0, 0))
    block = pl.BlockSpec((1, 4, CH, LAG_COUNT), lambda r, i: (r, i, 0, 0))
    dtype = BF16 if chunk == CHUNKS - 1 else F32
    return pl.pallas_call(
        functools.partial(invert_kernel, scaling, chunk),
        out_shape=jax.ShapeDtypeStruct((2, 8, CH, LAG_COUNT), dtype),
        grid=(2, 2),
        in_specs=[part] * 2
        + [pl.BlockSpec((2 * BINS, LAG_COUNT), lambda r, i: (0, 0))]
        + [block] * len(sums),
        out_specs=block,
        compiler_params=params(),
        cost_estimate=pl.CostEstimate(
            flops=1024 * 1024 * 1024, bytes_accessed=6 << 20, transcendentals=0
        ),
        name="invert",
    )(*parts, table, *sums)


def turns(freq_ids, delay_ids):
    angles = jnp.mod(freq_ids * delay_ids, WIN_SAMPLES).astype(F32) * (2.0 * math.pi / WIN_SAMPLES)
    return jnp.cos(angles), jnp.sin(angles)


def lag_table(core):
    n = lax.broadcasted_iota(jnp.int32, (BINS, 1), 0)
    fine = n % FC
    z = (n // FC) % 8
    part = (n // (8 * FC)) % 2
    chunk = n // (16 * FC)
    freq_ids = chunk * CBINS + z * (2 * FC) + (part ^ core) * FC + fine + BAND_START
    lane = lax.broadcasted_iota(jnp.int32, (BINS, 128), 1)
    coarse = lane % 8 * 128 - LAG_COUNT // 2
    return *turns(freq_ids, lane), *turns(freq_ids, coarse)


def table_kernel(cos_a, sin_a, cos_b, sin_b, *refs):
    out = refs[-1]
    ca, sa, cb, sb = cos_a[...], sin_a[...], cos_b[...], sin_b[...]
    for n in range(LAG_COUNT // 128):
        c, s = cb[:, n : n + 1], sb[:, n : n + 1]
        out[:BINS, n * 128 : n * 128 + 128] = (ca * c - sa * s).astype(BF16)
        out[BINS:, n * 128 : n * 128 + 128] = (-(sa * c + ca * s)).astype(BF16)


def join_table(parts):
    return pl.pallas_call(
        table_kernel,
        out_shape=jax.ShapeDtypeStruct((2 * BINS, LAG_COUNT), BF16),
        in_specs=[VM] * 4,
        out_specs=VM,
        compiler_params=params(),
        cost_estimate=pl.CostEstimate(flops=8 << 20, bytes_accessed=4 << 20, transcendentals=0),
        name="table",
    )(*parts)


def place(z):
    return (z % 2) * 4 + z // 2


def device(m, z, c):
    return (m % 16) * 16 + place(z % 8) * 2 + c


EVERY = [(m, z, c) for m in range(16) for z in range(8) for c in range(2)]


def send(value, target):
    return lax.ppermute(value, ALL, [(device(*d), device(*target(*d))) for d in EVERY])


def go_round(pieces):
    got = []
    for r in ORDER:
        got.append(send(pieces[r], lambda m, z, c: (m, z + r, c)) if r else pieces[r])
    return got


def back_round(pieces):
    got = []
    for r in ORDER:
        got.append(send(pieces[r], lambda m, z, c: (m + c, z + r, c)))
    return got


def other_core(value):
    return send(value, lambda m, z, c: (m, z, 1 - c))


def shards(spectra, valid_flags):
    z = 2 * lax.axis_index("zh") + lax.axis_index("zl")
    pos = jnp.stack([z, lax.axis_index("c")]).astype(jnp.int32)
    windows = spectra.shape[0] * lax.axis_size(("zh", "c"))
    scaling = 1.0 / math.sqrt(windows * BINS)
    flags2 = jnp.concatenate([valid_flags, valid_flags], axis=1)[:, None, :]
    *white, core = whiten(jnp.transpose(spectra, (2, 0, 1, 3)), flags2, pos)
    table = join_table(lag_table(core[0]))
    sums = ()
    merged, crossed = (table,), ()
    for k in range(CHUNKS):
        got = go_round(white[k * 8 : k * 8 + 8])
        same, other = merge(got, pos, *merged)
        prev0 = send(same, lambda m, z, c: (m + 1 - 2 * c, z, c))
        prev1 = send(other, lambda m, z, c: (m - 1 + 2 * c, z, 1 - c))
        own1 = other_core(other)
        out = cross(same, own1, prev0, prev1, pos, *crossed)
        crossed = merged = (out[0],)
        got = back_round(out)
        other = turn(1, got, pos, *sums)
        received = other_core(other)
        same = turn(0, got, pos, other)
        sums = (invert(k, [same, received], table, sums, scaling),)
    return sums[0]


def solution(mesh):
    grid = mesh.devices.reshape(4, 4, 2, 4, 2)
    fine = Mesh(grid, ("x", "y", "zl", "zh", "c"))
    blk, seg = ("x", "y", "zl"), ("zh", "c")
    in_specs = (P(seg, blk, None, None), P(seg, blk))
    out_specs = P(None, blk + seg, None, None)


    return jax.shard_map(shards, mesh=fine, in_specs=in_specs, out_specs=out_specs, check_vma=False)
```

```python
import functools
import math

import jax
import jax.numpy as jnp
from jax import lax
from jax.experimental import pallas as pl
from jax.experimental.pallas import tpu as pltpu
from jax.sharding import Mesh, PartitionSpec as P


LAG_COUNT = 1024
WIN_SAMPLES = 15000
BAND_START = 30
SMOOTH_HALF = 32
BINS = 512
WIN = 14
CH = 64
STEP = 2
CHUNKS = 2
FC = 32 // CHUNKS
CBINS = BINS // CHUNKS
ORDER = (0, 1, 7, 4, 3, 5, 2, 6)
F32 = jnp.float32
BF16 = jnp.bfloat16

ALL = ("x", "y", "zl", "zh", "c")
VM = pl.BlockSpec(memory_space=pltpu.VMEM)
SM = pl.BlockSpec(memory_space=pltpu.SMEM)
ANY = pl.BlockSpec(memory_space=pl.ANY)


def params():
    return pltpu.CompilerParams(vmem_limit_bytes=24 << 20)


def whiten_kernel(pos_ref, spec_ref, flags_ref, *refs):
    outs, core = refs[: 8 * CHUNKS], refs[8 * CHUNKS]
    band, eye, invc, white = refs[8 * CHUNKS + 1 :]
    w = pl.program_id(0)
    z, c = pos_ref[0], pos_ref[1]

    @pl.when(w == 0)
    def _():
        rows = lax.broadcasted_iota(jnp.int32, (BINS, BINS), 0)
        cols = lax.broadcasted_iota(jnp.int32, (BINS, BINS), 1)
        band[...] = jnp.where(jnp.abs(rows - cols) <= SMOOTH_HALF, 1.0, 0.0).astype(BF16)
        r2 = lax.broadcasted_iota(jnp.int32, (256, 256), 0)
        c2 = lax.broadcasted_iota(jnp.int32, (256, 256), 1)
        eye[...] = jnp.where(r2 == c2, 1.0, 0.0).astype(BF16)
        f = lax.broadcasted_iota(jnp.int32, (BINS, 128), 0)
        count = jnp.minimum(f + SMOOTH_HALF, BINS - 1) - jnp.maximum(f - SMOOTH_HALF, 0) + 1
        invc[...] = 1.0 / count.astype(F32)

    nt = (((1,), (1,)), ((), ()))
    for v in range(STEP):
        re16, im16 = spec_ref[0, v], spec_ref[1, v]
        re, im = re16.astype(F32), im16.astype(F32)
        amp = jnp.sqrt(re * re + im * im).astype(BF16)
        amp2 = jnp.concatenate([amp, amp], axis=0)
        both = jnp.concatenate([re16, im16], axis=0)
        summed = lax.dot_general(band[...], amp2, nt, preferred_element_type=F32)
        scale = flags_ref[v].astype(F32) / (summed * invc[...] + 1e-05)
        for h in range(2):
            half = lax.dot_general(
                eye[...], both[:, h * 256 : (h + 1) * 256], nt, preferred_element_type=F32
            )
            part = half * scale[h * 256 : (h + 1) * 256]
            white[v, h * 256 : (h + 1) * 256] = part.astype(BF16)
    for k in range(CHUNKS):
        for r in range(8):
            base = k * CBINS + ((z + r) & 7) * (2 * FC)
            for crel in range(2):
                start = pl.multiple_of(base + (c ^ crel) * FC, FC)
                for v in range(STEP):
                    outs[k * 8 + r][crel, w * STEP + v] = white[v, pl.ds(start, FC), :]
    core[0] = c


def whiten(spec, flags2, pos):
    shape = jax.ShapeDtypeStruct((2, WIN, FC, 128), BF16)
    full = pl.BlockSpec((2, WIN, FC, 128), lambda w, *_: (0, 0, 0, 0))
    return pl.pallas_call(
        whiten_kernel,
        out_shape=[shape] * (8 * CHUNKS) + [jax.ShapeDtypeStruct((1,), jnp.int32)],
        grid_spec=pltpu.PrefetchScalarGridSpec(
            num_scalar_prefetch=1,
            grid=(WIN // STEP,),
            in_specs=[
                pl.BlockSpec((2, STEP, CH, BINS), lambda w, *_: (0, w, 0, 0)),
                pl.BlockSpec((STEP, 1, 128), lambda w, *_: (w, 0, 0)),
            ],
            out_specs=[full] * (8 * CHUNKS) + [SM],
            scratch_shapes=[
                pltpu.VMEM((BINS, BINS), BF16),
                pltpu.VMEM((256, 256), BF16),
                pltpu.VMEM((BINS, 128), F32),
                pltpu.VMEM((STEP, BINS, 128), BF16),
            ],
        ),
        compiler_params=params(),
        cost_estimate=pl.CostEstimate(
            flops=3 * 512 * 512 * 128 * WIN, bytes_accessed=4 << 20, transcendentals=0
        ),
        name="whiten",
    )(pos, spec, flags2)


def merge_kernel(pos_ref, *refs):
    ins, (same, other) = refs[:8], refs[-2:]
    z = pos_ref[0]
    for n, r in enumerate(ORDER):
        src = (z - r) & 7
        same[src & 1, src >> 1] = ins[n][0]
        other[src & 1, src >> 1] = ins[n][1]


def merge(pieces, pos, *after):
    shape = jax.ShapeDtypeStruct((2, 4, WIN, FC, 128), BF16)
    return pl.pallas_call(
        merge_kernel,
        out_shape=[shape] * 2,
        in_specs=[SM] + [VM] * 8 + [ANY] * len(after),
        out_specs=[VM] * 2,
        compiler_params=params(),
        cost_estimate=pl.CostEstimate(
            flops=0, bytes_accessed=4 * 8 * WIN * FC * 256, transcendentals=0
        ),
        name="merge",
    )(pos, *pieces, *after)


def cross_kernel(pos_ref, own0, own1, prev0, prev1, *refs):
    outs, (wide, res) = refs[-10:-2], refs[-2:]
    z, c = pos_ref[0], pos_ref[1]
    rows = 4 * WIN * FC
    for n, (first, second) in enumerate(((own0, own1), (prev0, prev1))):
        for b in range(2):
            base = (n * 2 + b) * 2 * rows
            wide[base : base + rows] = first[b].reshape(rows, 128).astype(F32)
            wide[base + rows : base + 2 * rows] = second[b].reshape(rows, 128).astype(F32)
    sign = jnp.where(lax.broadcasted_iota(jnp.int32, (CH, 128), 1) < CH, 1.0, -1.0).astype(F32)
    tn = (((0,), (0,)), ((), ()))

    def one_bin(f, carry):
        x = [
            wide[pl.ds(n * 2 * rows + f, 8 * WIN, stride=FC), :].astype(BF16) for n in range(4)
        ]
        own_a, own_b, prev_a, prev_b = x
        for b, (left, rights) in enumerate(
            ((own_a, (prev_b, prev_a)), (own_b, (own_a, prev_b)))
        ):
            g = lax.dot_general(
                left, jnp.concatenate(rights, axis=1), tn, preferred_element_type=F32
            )
            for rnd in range(2):
                top = g[:CH, rnd * 128 : rnd * 128 + 128]
                bottom = pltpu.roll(g[CH:, rnd * 128 : rnd * 128 + 128], CH, 1)
                start = pl.multiple_of(((rnd * 2 + b) * FC + f) * CH, CH)
                res[pl.ds(start, CH), :] = bottom + sign * top
        return carry

    lax.fori_loop(0, FC, one_bin, 0, unroll=2)
    for r in range(8):
        dst = (z + r) & 7
        for crel in range(2):
            row = ((dst >> 1) * 2 + (c ^ crel)) * 8
            for rnd in range(2):
                base = (rnd * 2 + (dst & 1)) * FC * CH + row
                for i in range(8):
                    outs[r][crel, rnd, i] = res[pl.ds(base + i, FC, stride=CH), :].astype(BF16)


def cross(own0, own1, prev0, prev1, pos, *after):
    shape = jax.ShapeDtypeStruct((2, 2, 8, FC, 128), BF16)
    return pl.pallas_call(
        cross_kernel,
        out_shape=[shape] * 8,
        in_specs=[SM] + [VM] * 4 + [ANY] * len(after),
        out_specs=[VM] * 8,
        scratch_shapes=[
            pltpu.VMEM((32 * WIN * FC, 128), F32),
            pltpu.VMEM((4 * FC * CH, 128), F32),
        ],
        compiler_params=params(),
        cost_estimate=pl.CostEstimate(
            flops=4 * FC * 128 * 256 * 256, bytes_accessed=3 << 20, transcendentals=0
        ),
        name="cross",
    )(pos, own0, own1, prev0, prev1, *after)


def turn_kernel(pos_ref, *refs):
    ins, (out, buf) = refs[:8], refs[-2:]
    z = pos_ref[0]
    for rnd in range(2):
        for i in range(8):
            slot = i & 1
            for n, r in enumerate(ORDER):
                start = pl.multiple_of(((z - r) & 7) * FC, FC)
                buf[slot, pl.ds(start, FC), :] = ins[n][0, rnd, i].astype(F32)
            out[rnd, i] = buf[slot].T.astype(BF16)


def turn(crel, pieces, pos, *after):
    half = pl.BlockSpec((1, 2, 8, FC, 128), lambda n: (crel, 0, 0, 0, 0))
    whole = pl.BlockSpec((2, 8, 128, 8 * FC), lambda n: (0, 0, 0, 0))
    return pl.pallas_call(
        turn_kernel,
        out_shape=jax.ShapeDtypeStruct((2, 8, 128, 8 * FC), BF16),
        grid=(1,),
        in_specs=[SM] + [half] * 8 + [ANY] * len(after),
        out_specs=whole,
        scratch_shapes=[pltpu.VMEM((2, 8 * FC, 128), F32)],
        compiler_params=params(),
        cost_estimate=pl.CostEstimate(flops=0, bytes_accessed=2 << 20, transcendentals=0),
        name="turn",
    )(pos, *pieces, *after)


def invert_kernel(scaling, chunk, *refs):
    parts, table, sums, out = refs[:2], refs[2], refs[3:-1], refs[-1]
    total = 0.0
    for k in range(2):
        rows = []
        for i in range(4):
            cols = [p[0, i, k * CH : (k + 1) * CH] for p in parts]
            rows.append(jnp.concatenate(cols, axis=1))
        start = k * BINS + chunk * CBINS
        total += jnp.dot(
            jnp.concatenate(rows, axis=0),
            table[start : start + CBINS],
            preferred_element_type=F32,
        )
    total = total.reshape(4, CH, LAG_COUNT)
    for ref in sums:
        total += ref[0]
    if chunk == CHUNKS - 1:
        total = total * scaling
    out[0] = total.astype(out.dtype)


def invert(chunk, parts, table, sums, scaling):
    part = pl.BlockSpec((1, 4, 128, 8 * FC), lambda r, i: (r, i, 0, 0))
    block = pl.BlockSpec((1, 4, CH, LAG_COUNT), lambda r, i: (r, i, 0, 0))
    dtype = BF16 if chunk == CHUNKS - 1 else F32
    return pl.pallas_call(
        functools.partial(invert_kernel, scaling, chunk),
        out_shape=jax.ShapeDtypeStruct((2, 8, CH, LAG_COUNT), dtype),
        grid=(2, 2),
        in_specs=[part] * 2
        + [pl.BlockSpec((2 * BINS, LAG_COUNT), lambda r, i: (0, 0))]
        + [block] * len(sums),
        out_specs=block,
        compiler_params=params(),
        cost_estimate=pl.CostEstimate(
            flops=1024 * 1024 * 1024, bytes_accessed=6 << 20, transcendentals=0
        ),
        name="invert",
    )(*parts, table, *sums)


def turns(freq_ids, delay_ids):
    angles = jnp.mod(freq_ids * delay_ids, WIN_SAMPLES).astype(F32) * (2.0 * math.pi / WIN_SAMPLES)
    return jnp.cos(angles), jnp.sin(angles)


def lag_table(core):
    n = lax.broadcasted_iota(jnp.int32, (BINS, 1), 0)
    fine = n % FC
    z = (n // FC) % 8
    part = (n // (8 * FC)) % 2
    chunk = n // (16 * FC)
    freq_ids = chunk * CBINS + z * (2 * FC) + (part ^ core) * FC + fine + BAND_START
    lane = lax.broadcasted_iota(jnp.int32, (BINS, 128), 1)
    coarse = lane % 8 * 128 - LAG_COUNT // 2
    return *turns(freq_ids, lane), *turns(freq_ids, coarse)


def table_kernel(cos_a, sin_a, cos_b, sin_b, *refs):
    out = refs[-1]
    ca, sa, cb, sb = cos_a[...], sin_a[...], cos_b[...], sin_b[...]
    for n in range(LAG_COUNT // 128):
        c, s = cb[:, n : n + 1], sb[:, n : n + 1]
        out[:BINS, n * 128 : n * 128 + 128] = (ca * c - sa * s).astype(BF16)
        out[BINS:, n * 128 : n * 128 + 128] = (-(sa * c + ca * s)).astype(BF16)


def join_table(parts):
    return pl.pallas_call(
        table_kernel,
        out_shape=jax.ShapeDtypeStruct((2 * BINS, LAG_COUNT), BF16),
        in_specs=[VM] * 4,
        out_specs=VM,
        compiler_params=params(),
        cost_estimate=pl.CostEstimate(flops=8 << 20, bytes_accessed=4 << 20, transcendentals=0),
        name="table",
    )(*parts)


def place(z):
    return (z % 2) * 4 + z // 2


def device(m, z, c):
    return (m % 16) * 16 + place(z % 8) * 2 + c


EVERY = [(m, z, c) for m in range(16) for z in range(8) for c in range(2)]


def send(value, target):
    return lax.ppermute(value, ALL, [(device(*d), device(*target(*d))) for d in EVERY])


def round_ring(pieces):
    got = []
    for r in ORDER:
        got.append(send(pieces[r], lambda m, z, c: (m, z + r, c)) if r else pieces[r])
    return got


def other_core(value):
    return send(value, lambda m, z, c: (m, z, 1 - c))


def shards(spectra, valid_flags):
    z = 2 * lax.axis_index("zh") + lax.axis_index("zl")
    pos = jnp.stack([z, lax.axis_index("c")]).astype(jnp.int32)
    windows = spectra.shape[0] * lax.axis_size(("zh", "c"))
    scaling = 1.0 / math.sqrt(windows * BINS)
    flags2 = jnp.concatenate([valid_flags, valid_flags], axis=1)[:, None, :]
    *white, core = whiten(jnp.transpose(spectra, (2, 0, 1, 3)), flags2, pos)
    table = join_table(lag_table(core[0]))
    sums = ()
    merged, crossed = (table,), ()
    for k in range(CHUNKS):
        got = round_ring(white[k * 8 : k * 8 + 8])
        same, other = merge(got, pos, *merged)
        merged = (same,)
        prev0 = send(same, lambda m, z, c: (m + 1, z, c))
        prev1 = send(other, lambda m, z, c: (m + 1, z, 1 - c))
        own1 = other_core(other)
        out = cross(same, own1, prev0, prev1, pos, *crossed)
        crossed = (out[0],)
        got = round_ring(out)
        other = turn(1, got, pos, *sums)
        received = other_core(other)
        same = turn(0, got, pos, other)
        sums = (invert(k, [same, received], table, sums, scaling),)
    return sums[0]


def solution(mesh):
    grid = mesh.devices.reshape(4, 4, 2, 4, 2)
    fine = Mesh(grid, ("x", "y", "zl", "zh", "c"))
    blk, seg = ("x", "y", "zl"), ("zh", "c")
    in_specs = (P(seg, blk, None, None), P(seg, blk))
    out_specs = P(None, blk + seg, None, None)


    return jax.shard_map(shards, mesh=fine, in_specs=in_specs, out_specs=out_specs, check_vma=False)
```

```python
import functools
import math

import jax
import jax.numpy as jnp
from jax import lax
from jax.experimental import pallas as pl
from jax.experimental.pallas import tpu as pltpu
from jax.sharding import Mesh, PartitionSpec as P


LAG_COUNT = 1024
WIN_SAMPLES = 15000
BAND_START = 30
SMOOTH_HALF = 32
BINS = 512
WIN = 14
CH = 64
STEP = 2
CHUNKS = 2
FC = 32 // CHUNKS
CBINS = BINS // CHUNKS
ORDER = (0, 1, 7, 4, 3, 5, 2, 6)
F32 = jnp.float32
BF16 = jnp.bfloat16

ALL = ("x", "y", "zl", "zh", "c")
VM = pl.BlockSpec(memory_space=pltpu.VMEM)
SM = pl.BlockSpec(memory_space=pltpu.SMEM)
ANY = pl.BlockSpec(memory_space=pl.ANY)


def params():
    return pltpu.CompilerParams(vmem_limit_bytes=24 << 20)


def whiten_kernel(pos_ref, spec_ref, flags_ref, *refs):
    outs, core = refs[: 8 * CHUNKS], refs[8 * CHUNKS]
    band, eye, invc, white = refs[8 * CHUNKS + 1 :]
    w = pl.program_id(0)
    z, c = pos_ref[0], pos_ref[1]

    @pl.when(w == 0)
    def _():
        rows = lax.broadcasted_iota(jnp.int32, (BINS, BINS), 0)
        cols = lax.broadcasted_iota(jnp.int32, (BINS, BINS), 1)
        band[...] = jnp.where(jnp.abs(rows - cols) <= SMOOTH_HALF, 1.0, 0.0).astype(BF16)
        r2 = lax.broadcasted_iota(jnp.int32, (256, 256), 0)
        c2 = lax.broadcasted_iota(jnp.int32, (256, 256), 1)
        eye[...] = jnp.where(r2 == c2, 1.0, 0.0).astype(BF16)
        f = lax.broadcasted_iota(jnp.int32, (BINS, 128), 0)
        count = jnp.minimum(f + SMOOTH_HALF, BINS - 1) - jnp.maximum(f - SMOOTH_HALF, 0) + 1
        invc[...] = 1.0 / count.astype(F32)

    nt = (((1,), (1,)), ((), ()))
    for v in range(STEP):
        re16, im16 = spec_ref[0, v], spec_ref[1, v]
        re, im = re16.astype(F32), im16.astype(F32)
        amp = jnp.sqrt(re * re + im * im).astype(BF16)
        amp2 = jnp.concatenate([amp, amp], axis=0)
        both = jnp.concatenate([re16, im16], axis=0)
        summed = lax.dot_general(band[...], amp2, nt, preferred_element_type=F32)
        flags = flags_ref[pl.ds(w * STEP + v, 1), :].astype(F32)
        flags = jnp.concatenate([flags, flags], axis=1)
        scale = flags / (summed * invc[...] + 1e-05)
        for h in range(2):
            half = lax.dot_general(
                eye[...], both[:, h * 256 : (h + 1) * 256], nt, preferred_element_type=F32
            )
            part = half * scale[h * 256 : (h + 1) * 256]
            white[v, h * 256 : (h + 1) * 256] = part.astype(BF16)
    for k in range(CHUNKS):
        for r in range(8):
            base = k * CBINS + ((z + r) & 7) * (2 * FC)
            for crel in range(2):
                start = pl.multiple_of(base + (c ^ crel) * FC, FC)
                for v in range(STEP):
                    outs[k * 8 + r][crel, w * STEP + v] = white[v, pl.ds(start, FC), :]
    core[0] = c


def whiten(spec, valid_flags, pos):
    shape = jax.ShapeDtypeStruct((2, WIN, FC, 128), BF16)
    full = pl.BlockSpec((2, WIN, FC, 128), lambda w, *_: (0, 0, 0, 0))
    return pl.pallas_call(
        whiten_kernel,
        out_shape=[shape] * (8 * CHUNKS) + [jax.ShapeDtypeStruct((1,), jnp.int32)],
        grid_spec=pltpu.PrefetchScalarGridSpec(
            num_scalar_prefetch=1,
            grid=(WIN // STEP,),
            in_specs=[
                pl.BlockSpec((2, STEP, CH, BINS), lambda w, *_: (0, w, 0, 0)),
                pl.BlockSpec((WIN, CH), lambda w, *_: (0, 0)),
            ],
            out_specs=[full] * (8 * CHUNKS) + [SM],
            scratch_shapes=[
                pltpu.VMEM((BINS, BINS), BF16),
                pltpu.VMEM((256, 256), BF16),
                pltpu.VMEM((BINS, 128), F32),
                pltpu.VMEM((STEP, BINS, 128), BF16),
            ],
        ),
        compiler_params=params(),
        cost_estimate=pl.CostEstimate(
            flops=3 * 512 * 512 * 128 * WIN, bytes_accessed=4 << 20, transcendentals=0
        ),
        name="whiten",
    )(pos, spec, valid_flags)


def merge_kernel(pos_ref, *refs):
    ins, (same, other) = refs[:8], refs[-2:]
    z = pos_ref[0]
    for n, r in enumerate(ORDER):
        src = (z - r) & 7
        same[src & 1, src >> 1] = ins[n][0]
        other[src & 1, src >> 1] = ins[n][1]


def merge(pieces, pos, *after):
    shape = jax.ShapeDtypeStruct((2, 4, WIN, FC, 128), BF16)
    return pl.pallas_call(
        merge_kernel,
        out_shape=[shape] * 2,
        in_specs=[SM] + [VM] * 8 + [ANY] * len(after),
        out_specs=[VM] * 2,
        compiler_params=params(),
        cost_estimate=pl.CostEstimate(
            flops=0, bytes_accessed=4 * 8 * WIN * FC * 256, transcendentals=0
        ),
        name="merge",
    )(pos, *pieces, *after)


def cross_kernel(pos_ref, own0, own1, prev0, prev1, *refs):
    outs, (wide, res) = refs[-10:-2], refs[-2:]
    z, c = pos_ref[0], pos_ref[1]
    rows = 4 * WIN * FC
    for n, (first, second) in enumerate(((own0, own1), (prev0, prev1))):
        for b in range(2):
            base = (n * 2 + b) * 2 * rows
            wide[base : base + rows] = first[b].reshape(rows, 128).astype(F32)
            wide[base + rows : base + 2 * rows] = second[b].reshape(rows, 128).astype(F32)
    sign = jnp.where(lax.broadcasted_iota(jnp.int32, (CH, 128), 1) < CH, 1.0, -1.0).astype(F32)
    tn = (((0,), (0,)), ((), ()))

    def one_bin(f, carry):
        x = [
            wide[pl.ds(n * 2 * rows + f, 8 * WIN, stride=FC), :].astype(BF16) for n in range(4)
        ]
        own_a, own_b, prev_a, prev_b = x
        for b, (left, rights) in enumerate(
            ((own_a, (prev_b, prev_a)), (own_b, (own_a, prev_b)))
        ):
            g = lax.dot_general(
                left, jnp.concatenate(rights, axis=1), tn, preferred_element_type=F32
            )
            for rnd in range(2):
                top = g[:CH, rnd * 128 : rnd * 128 + 128]
                bottom = pltpu.roll(g[CH:, rnd * 128 : rnd * 128 + 128], CH, 1)
                start = pl.multiple_of(((rnd * 2 + b) * FC + f) * CH, CH)
                res[pl.ds(start, CH), :] = bottom + sign * top
        return carry

    lax.fori_loop(0, FC, one_bin, 0, unroll=2)
    for r in range(8):
        dst = (z + r) & 7
        for crel in range(2):
            row = ((dst >> 1) * 2 + (c ^ crel)) * 8
            for rnd in range(2):
                base = (rnd * 2 + (dst & 1)) * FC * CH + row
                for i in range(8):
                    outs[r][crel, rnd, i] = res[pl.ds(base + i, FC, stride=CH), :].astype(BF16)


def cross(own0, own1, prev0, prev1, pos, *after):
    shape = jax.ShapeDtypeStruct((2, 2, 8, FC, 128), BF16)
    return pl.pallas_call(
        cross_kernel,
        out_shape=[shape] * 8,
        in_specs=[SM] + [VM] * 4 + [ANY] * len(after),
        out_specs=[VM] * 8,
        scratch_shapes=[
            pltpu.VMEM((32 * WIN * FC, 128), F32),
            pltpu.VMEM((4 * FC * CH, 128), F32),
        ],
        compiler_params=params(),
        cost_estimate=pl.CostEstimate(
            flops=4 * FC * 128 * 256 * 256, bytes_accessed=3 << 20, transcendentals=0
        ),
        name="cross",
    )(pos, own0, own1, prev0, prev1, *after)


def turn_kernel(pos_ref, *refs):
    ins, (out, buf) = refs[:8], refs[-2:]
    z = pos_ref[0]
    for rnd in range(2):
        for i in range(8):
            slot = i & 1
            for n, r in enumerate(ORDER):
                start = pl.multiple_of(((z - r) & 7) * FC, FC)
                buf[slot, pl.ds(start, FC), :] = ins[n][0, rnd, i].astype(F32)
            out[rnd, i] = buf[slot].T.astype(BF16)


def turn(crel, pieces, pos, *after):
    half = pl.BlockSpec((1, 2, 8, FC, 128), lambda n: (crel, 0, 0, 0, 0))
    whole = pl.BlockSpec((2, 8, 128, 8 * FC), lambda n: (0, 0, 0, 0))
    return pl.pallas_call(
        turn_kernel,
        out_shape=jax.ShapeDtypeStruct((2, 8, 128, 8 * FC), BF16),
        grid=(1,),
        in_specs=[SM] + [half] * 8 + [ANY] * len(after),
        out_specs=whole,
        scratch_shapes=[pltpu.VMEM((2, 8 * FC, 128), F32)],
        compiler_params=params(),
        cost_estimate=pl.CostEstimate(flops=0, bytes_accessed=2 << 20, transcendentals=0),
        name="turn",
    )(pos, *pieces, *after)


def invert_kernel(scaling, chunk, *refs):
    parts, table, sums, out = refs[:2], refs[2], refs[3:-1], refs[-1]
    total = 0.0
    for k in range(2):
        rows = []
        for i in range(4):
            cols = [p[0, i, k * CH : (k + 1) * CH] for p in parts]
            rows.append(jnp.concatenate(cols, axis=1))
        start = k * BINS + chunk * CBINS
        total += jnp.dot(
            jnp.concatenate(rows, axis=0),
            table[start : start + CBINS],
            preferred_element_type=F32,
        )
    total = total.reshape(4, CH, LAG_COUNT)
    for ref in sums:
        total += ref[0]
    if chunk == CHUNKS - 1:
        total = total * scaling
    out[0] = total.astype(out.dtype)


def invert(chunk, parts, table, sums, scaling):
    part = pl.BlockSpec((1, 4, 128, 8 * FC), lambda r, i: (r, i, 0, 0))
    block = pl.BlockSpec((1, 4, CH, LAG_COUNT), lambda r, i: (r, i, 0, 0))
    dtype = BF16 if chunk == CHUNKS - 1 else F32
    return pl.pallas_call(
        functools.partial(invert_kernel, scaling, chunk),
        out_shape=jax.ShapeDtypeStruct((2, 8, CH, LAG_COUNT), dtype),
        grid=(2, 2),
        in_specs=[part] * 2
        + [pl.BlockSpec((2 * BINS, LAG_COUNT), lambda r, i: (0, 0))]
        + [block] * len(sums),
        out_specs=block,
        compiler_params=params(),
        cost_estimate=pl.CostEstimate(
            flops=1024 * 1024 * 1024, bytes_accessed=6 << 20, transcendentals=0
        ),
        name="invert",
    )(*parts, table, *sums)


def turns(freq_ids, delay_ids):
    angles = jnp.mod(freq_ids * delay_ids, WIN_SAMPLES).astype(F32) * (2.0 * math.pi / WIN_SAMPLES)
    return jnp.cos(angles), jnp.sin(angles)


def lag_table(core):
    n = lax.broadcasted_iota(jnp.int32, (BINS, 1), 0)
    fine = n % FC
    z = (n // FC) % 8
    part = (n // (8 * FC)) % 2
    chunk = n // (16 * FC)
    freq_ids = chunk * CBINS + z * (2 * FC) + (part ^ core) * FC + fine + BAND_START
    lane = lax.broadcasted_iota(jnp.int32, (BINS, 128), 1)
    coarse = lane % 8 * 128 - LAG_COUNT // 2
    return *turns(freq_ids, lane), *turns(freq_ids, coarse)


def table_kernel(cos_a, sin_a, cos_b, sin_b, *refs):
    out = refs[-1]
    ca, sa, cb, sb = cos_a[...], sin_a[...], cos_b[...], sin_b[...]
    for n in range(LAG_COUNT // 128):
        c, s = cb[:, n : n + 1], sb[:, n : n + 1]
        out[:BINS, n * 128 : n * 128 + 128] = (ca * c - sa * s).astype(BF16)
        out[BINS:, n * 128 : n * 128 + 128] = (-(sa * c + ca * s)).astype(BF16)


def join_table(parts):
    return pl.pallas_call(
        table_kernel,
        out_shape=jax.ShapeDtypeStruct((2 * BINS, LAG_COUNT), BF16),
        in_specs=[VM] * 4,
        out_specs=VM,
        compiler_params=params(),
        cost_estimate=pl.CostEstimate(flops=8 << 20, bytes_accessed=4 << 20, transcendentals=0),
        name="table",
    )(*parts)


def place(z):
    return (z % 2) * 4 + z // 2


def device(m, z, c):
    return (m % 16) * 16 + place(z % 8) * 2 + c


EVERY = [(m, z, c) for m in range(16) for z in range(8) for c in range(2)]


def send(value, target):
    return lax.ppermute(value, ALL, [(device(*d), device(*target(*d))) for d in EVERY])


def round_ring(pieces):
    got = []
    for r in ORDER:
        got.append(send(pieces[r], lambda m, z, c: (m, z + r, c)) if r else pieces[r])
    return got


def other_core(value):
    return send(value, lambda m, z, c: (m, z, 1 - c))


def shards(spectra, valid_flags):
    z = 2 * lax.axis_index("zh") + lax.axis_index("zl")
    pos = jnp.stack([z, lax.axis_index("c")]).astype(jnp.int32)
    windows = spectra.shape[0] * lax.axis_size(("zh", "c"))
    scaling = 1.0 / math.sqrt(windows * BINS)
    *white, core = whiten(jnp.transpose(spectra, (2, 0, 1, 3)), valid_flags, pos)
    table = join_table(lag_table(core[0]))
    sums = ()
    merged, crossed = (), ()
    for k in range(CHUNKS):
        got = round_ring(white[k * 8 : k * 8 + 8])
        same, other = merge(got, pos, *merged)
        merged = (same, table)
        prev0 = send(same, lambda m, z, c: (m + 1, z, c))
        prev1 = send(other, lambda m, z, c: (m + 1, z, 1 - c))
        own1 = other_core(other)
        out = cross(same, own1, prev0, prev1, pos, *crossed)
        crossed = (out[0],)
        got = round_ring(out)
        other = turn(1, got, pos, *sums)
        received = other_core(other)
        same = turn(0, got, pos, other)
        sums = (invert(k, [same, received], table, sums, scaling),)
    return sums[0]


def solution(mesh):
    grid = mesh.devices.reshape(4, 4, 2, 4, 2)
    fine = Mesh(grid, ("x", "y", "zl", "zh", "c"))
    blk, seg = ("x", "y", "zl"), ("zh", "c")
    in_specs = (P(seg, blk, None, None), P(seg, blk))
    out_specs = P(None, blk + seg, None, None)


    return jax.shard_map(shards, mesh=fine, in_specs=in_specs, out_specs=out_specs, check_vma=False)
```

```python
import functools
import math

import jax
import jax.numpy as jnp
from jax import lax
from jax.experimental import pallas as pl
from jax.experimental.pallas import tpu as pltpu
from jax.sharding import Mesh, PartitionSpec as P


LAG_COUNT = 1024
WIN_SAMPLES = 15000
BAND_START = 30
SMOOTH_HALF = 32
BINS = 512
WIN = 14
CH = 64
STEP = 2
CHUNKS = 2
FC = 32 // CHUNKS
CBINS = BINS // CHUNKS
ORDER = (0, 1, 7, 4, 3, 5, 2, 6)
F32 = jnp.float32
BF16 = jnp.bfloat16

ALL = ("x", "y", "zl", "zh", "c")
VM = pl.BlockSpec(memory_space=pltpu.VMEM)
SM = pl.BlockSpec(memory_space=pltpu.SMEM)
ANY = pl.BlockSpec(memory_space=pl.ANY)


def params():
    return pltpu.CompilerParams(vmem_limit_bytes=24 << 20)


def whiten_kernel(pos_ref, spec_ref, flags_ref, *refs):
    outs, core = refs[: 8 * CHUNKS], refs[8 * CHUNKS]
    band, eye, invc, white = refs[8 * CHUNKS + 1 :]
    w = pl.program_id(0)
    z, c = pos_ref[0], pos_ref[1]

    @pl.when(w == 0)
    def _():
        rows = lax.broadcasted_iota(jnp.int32, (BINS, BINS), 0)
        cols = lax.broadcasted_iota(jnp.int32, (BINS, BINS), 1)
        band[...] = jnp.where(jnp.abs(rows - cols) <= SMOOTH_HALF, 1.0, 0.0).astype(BF16)
        r2 = lax.broadcasted_iota(jnp.int32, (256, 256), 0)
        c2 = lax.broadcasted_iota(jnp.int32, (256, 256), 1)
        eye[...] = jnp.where(r2 == c2, 1.0, 0.0).astype(BF16)
        f = lax.broadcasted_iota(jnp.int32, (BINS, 128), 0)
        count = jnp.minimum(f + SMOOTH_HALF, BINS - 1) - jnp.maximum(f - SMOOTH_HALF, 0) + 1
        invc[...] = 1.0 / count.astype(F32)

    nt = (((1,), (1,)), ((), ()))
    for v in range(STEP):
        re16, im16 = spec_ref[0, v], spec_ref[1, v]
        re, im = re16.astype(F32), im16.astype(F32)
        amp = jnp.sqrt(re * re + im * im).astype(BF16)
        amp2 = jnp.concatenate([amp, amp], axis=0)
        both = jnp.concatenate([re16, im16], axis=0)
        summed = lax.dot_general(band[...], amp2, nt, preferred_element_type=F32)
        flags = flags_ref[pl.ds(w * STEP + v, 1), :].astype(F32)
        flags = jnp.concatenate([flags, flags], axis=1)
        scale = flags / (summed * invc[...] + 1e-05)
        for h in range(2):
            half = lax.dot_general(
                eye[...], both[:, h * 256 : (h + 1) * 256], nt, preferred_element_type=F32
            )
            part = half * scale[h * 256 : (h + 1) * 256]
            white[v, h * 256 : (h + 1) * 256] = part.astype(BF16)
    for k in range(CHUNKS):
        for r in range(8):
            base = k * CBINS + ((z + r) & 7) * (2 * FC)
            for crel in range(2):
                start = pl.multiple_of(base + (c ^ crel) * FC, FC)
                for v in range(STEP):
                    outs[k * 8 + r][crel, w * STEP + v] = white[v, pl.ds(start, FC), :]
    core[0] = c


def whiten(spec, valid_flags, pos):
    shape = jax.ShapeDtypeStruct((2, WIN, FC, 128), BF16)
    full = pl.BlockSpec((2, WIN, FC, 128), lambda w, *_: (0, 0, 0, 0))
    return pl.pallas_call(
        whiten_kernel,
        out_shape=[shape] * (8 * CHUNKS) + [jax.ShapeDtypeStruct((1,), jnp.int32)],
        grid_spec=pltpu.PrefetchScalarGridSpec(
            num_scalar_prefetch=1,
            grid=(WIN // STEP,),
            in_specs=[
                pl.BlockSpec((2, STEP, CH, BINS), lambda w, *_: (0, w, 0, 0)),
                pl.BlockSpec((WIN, CH), lambda w, *_: (0, 0)),
            ],
            out_specs=[full] * (8 * CHUNKS) + [SM],
            scratch_shapes=[
                pltpu.VMEM((BINS, BINS), BF16),
                pltpu.VMEM((256, 256), BF16),
                pltpu.VMEM((BINS, 128), F32),
                pltpu.VMEM((STEP, BINS, 128), BF16),
            ],
        ),
        compiler_params=params(),
        cost_estimate=pl.CostEstimate(
            flops=3 * 512 * 512 * 128 * WIN, bytes_accessed=4 << 20, transcendentals=0
        ),
        name="whiten",
    )(pos, spec, valid_flags)


def merge_kernel(pos_ref, *refs):
    ins, (same, other) = refs[:8], refs[-2:]
    z = pos_ref[0]
    for n, r in enumerate(ORDER):
        src = (z - r) & 7
        same[src & 1, src >> 1] = ins[n][0]
        other[src & 1, src >> 1] = ins[n][1]


def merge(pieces, pos, *after):
    shape = jax.ShapeDtypeStruct((2, 4, WIN, FC, 128), BF16)
    return pl.pallas_call(
        merge_kernel,
        out_shape=[shape] * 2,
        in_specs=[SM] + [VM] * 8 + [ANY] * len(after),
        out_specs=[VM] * 2,
        compiler_params=params(),
        cost_estimate=pl.CostEstimate(
            flops=0, bytes_accessed=4 * 8 * WIN * FC * 256, transcendentals=0
        ),
        name="merge",
    )(pos, *pieces, *after)


def cross_kernel(pos_ref, own0, own1, prev0, prev1, *refs):
    outs, (wide, res) = refs[-10:-2], refs[-2:]
    z, c = pos_ref[0], pos_ref[1]
    rows = 4 * WIN * FC
    for n, (first, second) in enumerate(((own0, own1), (prev0, prev1))):
        for b in range(2):
            base = (n * 2 + b) * 2 * rows
            wide[base : base + rows] = first[b].reshape(rows, 128).astype(F32)
            wide[base + rows : base + 2 * rows] = second[b].reshape(rows, 128).astype(F32)
    sign = jnp.where(lax.broadcasted_iota(jnp.int32, (CH, 128), 1) < CH, 1.0, -1.0).astype(F32)
    tn = (((0,), (0,)), ((), ()))

    def one_bin(f, carry):
        x = [
            wide[pl.ds(n * 2 * rows + f, 8 * WIN, stride=FC), :].astype(BF16) for n in range(4)
        ]
        own_a, own_b, prev_a, prev_b = x
        for b, (left, rights) in enumerate(
            ((own_a, (prev_b, prev_a)), (own_b, (own_a, prev_b)))
        ):
            g = lax.dot_general(
                left, jnp.concatenate(rights, axis=1), tn, preferred_element_type=F32
            )
            for rnd in range(2):
                top = g[:CH, rnd * 128 : rnd * 128 + 128]
                bottom = pltpu.roll(g[CH:, rnd * 128 : rnd * 128 + 128], CH, 1)
                start = pl.multiple_of(((rnd * 2 + b) * FC + f) * CH, CH)
                res[pl.ds(start, CH), :] = bottom + sign * top
        return carry

    lax.fori_loop(0, FC, one_bin, 0, unroll=4)
    for r in range(8):
        dst = (z + r) & 7
        for crel in range(2):
            row = ((dst >> 1) * 2 + (c ^ crel)) * 8
            for rnd in range(2):
                base = (rnd * 2 + (dst & 1)) * FC * CH + row
                for i in range(8):
                    outs[r][crel, rnd, i] = res[pl.ds(base + i, FC, stride=CH), :].astype(BF16)


def cross(own0, own1, prev0, prev1, pos, *after):
    shape = jax.ShapeDtypeStruct((2, 2, 8, FC, 128), BF16)
    return pl.pallas_call(
        cross_kernel,
        out_shape=[shape] * 8,
        in_specs=[SM] + [VM] * 4 + [ANY] * len(after),
        out_specs=[VM] * 8,
        scratch_shapes=[
            pltpu.VMEM((32 * WIN * FC + FC, 128), F32),
            pltpu.VMEM((4 * FC * CH + CH, 128), F32),
        ],
        compiler_params=params(),
        cost_estimate=pl.CostEstimate(
            flops=4 * FC * 128 * 256 * 256, bytes_accessed=3 << 20, transcendentals=0
        ),
        name="cross",
    )(pos, own0, own1, prev0, prev1, *after)


def turn_kernel(pos_ref, *refs):
    ins, (out, buf) = refs[:8], refs[-2:]
    z = pos_ref[0]

    @pl.loop(0, 2)
    def _(rnd):
        for i in range(8):
            slot = i & 1
            for n, r in enumerate(ORDER):
                start = pl.multiple_of(((z - r) & 7) * FC, FC)
                buf[slot, pl.ds(start, FC), :] = ins[n][0, rnd, i].astype(F32)
            out[rnd, i] = buf[slot].T.astype(BF16)


def turn(crel, pieces, pos, *after):
    half = pl.BlockSpec((1, 2, 8, FC, 128), lambda n: (crel, 0, 0, 0, 0))
    whole = pl.BlockSpec((2, 8, 128, 8 * FC), lambda n: (0, 0, 0, 0))
    return pl.pallas_call(
        turn_kernel,
        out_shape=jax.ShapeDtypeStruct((2, 8, 128, 8 * FC), BF16),
        grid=(1,),
        in_specs=[SM] + [half] * 8 + [ANY] * len(after),
        out_specs=whole,
        scratch_shapes=[pltpu.VMEM((2, 8 * FC, 128), F32)],
        compiler_params=params(),
        cost_estimate=pl.CostEstimate(flops=0, bytes_accessed=2 << 20, transcendentals=0),
        name="turn",
    )(pos, *pieces, *after)


def invert_kernel(scaling, chunk, *refs):
    parts, table, sums, out = refs[:2], refs[2], refs[3:-1], refs[-1]
    total = 0.0
    for k in range(2):
        rows = []
        for i in range(4):
            cols = [p[0, i, k * CH : (k + 1) * CH] for p in parts]
            rows.append(jnp.concatenate(cols, axis=1))
        total += jnp.dot(
            jnp.concatenate(rows, axis=0), table[k], preferred_element_type=F32
        )
    total = total.reshape(4, CH, LAG_COUNT)
    for ref in sums:
        total += ref[0]
    if chunk == CHUNKS - 1:
        total = total * scaling
    out[0] = total.astype(out.dtype)


def invert(chunk, parts, table, sums, scaling):
    part = pl.BlockSpec((1, 4, 128, 8 * FC), lambda r, i: (r, i, 0, 0))
    block = pl.BlockSpec((1, 4, CH, LAG_COUNT), lambda r, i: (r, i, 0, 0))
    dtype = BF16 if chunk == CHUNKS - 1 else F32
    return pl.pallas_call(
        functools.partial(invert_kernel, scaling, chunk),
        out_shape=jax.ShapeDtypeStruct((2, 8, CH, LAG_COUNT), dtype),
        grid=(2, 2),
        in_specs=[part] * 2
        + [pl.BlockSpec((2, CBINS, LAG_COUNT), lambda r, i: (0, chunk, 0))]
        + [block] * len(sums),
        out_specs=block,
        compiler_params=params(),
        cost_estimate=pl.CostEstimate(
            flops=1024 * 1024 * 1024, bytes_accessed=6 << 20, transcendentals=0
        ),
        name="invert",
    )(*parts, table.reshape(2, BINS, LAG_COUNT), *sums)


def turns(freq_ids, delay_ids):
    angles = jnp.mod(freq_ids * delay_ids, WIN_SAMPLES).astype(F32) * (2.0 * math.pi / WIN_SAMPLES)
    return jnp.cos(angles), jnp.sin(angles)


def lag_table(core):
    n = lax.broadcasted_iota(jnp.int32, (BINS, 1), 0)
    fine = n % FC
    z = (n // FC) % 8
    part = (n // (8 * FC)) % 2
    chunk = n // (16 * FC)
    freq_ids = chunk * CBINS + z * (2 * FC) + (part ^ core) * FC + fine + BAND_START
    lane = lax.broadcasted_iota(jnp.int32, (BINS, 128), 1)
    coarse = lane % 8 * 128 - LAG_COUNT // 2
    return *turns(freq_ids, lane), *turns(freq_ids, coarse)


def table_kernel(cos_a, sin_a, cos_b, sin_b, *refs):
    out = refs[-1]
    ca, sa, cb, sb = cos_a[...], sin_a[...], cos_b[...], sin_b[...]
    for n in range(LAG_COUNT // 128):
        c, s = cb[:, n : n + 1], sb[:, n : n + 1]
        out[:BINS, n * 128 : n * 128 + 128] = (ca * c - sa * s).astype(BF16)
        out[BINS:, n * 128 : n * 128 + 128] = (-(sa * c + ca * s)).astype(BF16)


def join_table(parts):
    return pl.pallas_call(
        table_kernel,
        out_shape=jax.ShapeDtypeStruct((2 * BINS, LAG_COUNT), BF16),
        in_specs=[VM] * 4,
        out_specs=VM,
        compiler_params=params(),
        cost_estimate=pl.CostEstimate(flops=8 << 20, bytes_accessed=4 << 20, transcendentals=0),
        name="table",
    )(*parts)


def place(z):
    return (z % 2) * 4 + z // 2


def device(m, z, c):
    return (m % 16) * 16 + place(z % 8) * 2 + c


EVERY = [(m, z, c) for m in range(16) for z in range(8) for c in range(2)]


def send(value, target):
    return lax.ppermute(value, ALL, [(device(*d), device(*target(*d))) for d in EVERY])


def round_ring(pieces):
    got = []
    for r in ORDER:
        got.append(send(pieces[r], lambda m, z, c: (m, z + r, c)) if r else pieces[r])
    return got


def other_core(value):
    return send(value, lambda m, z, c: (m, z, 1 - c))


def shards(spectra, valid_flags):
    z = 2 * lax.axis_index("zh") + lax.axis_index("zl")
    pos = jnp.stack([z, lax.axis_index("c")]).astype(jnp.int32)
    windows = spectra.shape[0] * lax.axis_size(("zh", "c"))
    scaling = 1.0 / math.sqrt(windows * BINS)
    *white, core = whiten(jnp.transpose(spectra, (2, 0, 1, 3)), valid_flags, pos)
    table = join_table(lag_table(core[0]))
    sums = ()
    merged, crossed = (), ()
    for k in range(CHUNKS):
        got = round_ring(white[k * 8 : k * 8 + 8])
        same, other = merge(got, pos, *merged)
        merged = (same, table)
        prev0 = send(same, lambda m, z, c: (m + 1, z, c))
        prev1 = send(other, lambda m, z, c: (m + 1, z, 1 - c))
        own1 = other_core(other)
        out = cross(same, own1, prev0, prev1, pos, *crossed)
        crossed = (out[0],)
        got = round_ring(out)
        other = turn(1, got, pos, *sums)
        received = other_core(other)
        same = turn(0, got, pos, other)
        sums = (invert(k, [same, received], table, sums, scaling),)
    return sums[0]


def solution(mesh):
    grid = mesh.devices.reshape(4, 4, 2, 4, 2)
    fine = Mesh(grid, ("x", "y", "zl", "zh", "c"))
    blk, seg = ("x", "y", "zl"), ("zh", "c")
    in_specs = (P(seg, blk, None, None), P(seg, blk))
    out_specs = P(None, blk + seg, None, None)


    return jax.shard_map(shards, mesh=fine, in_specs=in_specs, out_specs=out_specs, check_vma=False)
```

```python
import functools
import math

import jax
import jax.numpy as jnp
from jax import lax
from jax.experimental import pallas as pl
from jax.experimental.pallas import tpu as pltpu
from jax.sharding import Mesh, PartitionSpec as P


LAG_COUNT = 1024
WIN_SAMPLES = 15000
BAND_START = 30
SMOOTH_HALF = 32
BINS = 512
WIN = 14
CH = 64
STEP = 2
CHUNKS = 2
FC = 32 // CHUNKS
CBINS = BINS // CHUNKS
ORDER = (0, 1, 7, 4, 3, 5, 2, 6)
FAR = (0, 4, 3, 5, 2, 6, 1, 7)
F32 = jnp.float32
BF16 = jnp.bfloat16

ALL = ("x", "y", "zl", "zh", "c")
VM = pl.BlockSpec(memory_space=pltpu.VMEM)
SM = pl.BlockSpec(memory_space=pltpu.SMEM)
ANY = pl.BlockSpec(memory_space=pl.ANY)


def params():
    return pltpu.CompilerParams(vmem_limit_bytes=24 << 20)


def whiten_kernel(pos_ref, spec_ref, flags_ref, *refs):
    outs, core = refs[: 8 * CHUNKS], refs[8 * CHUNKS]
    band, eye, invc, white = refs[8 * CHUNKS + 1 :]
    w = pl.program_id(0)
    z, c = pos_ref[0], pos_ref[1]

    @pl.when(w == 0)
    def _():
        rows = lax.broadcasted_iota(jnp.int32, (BINS, BINS), 0)
        cols = lax.broadcasted_iota(jnp.int32, (BINS, BINS), 1)
        band[...] = jnp.where(jnp.abs(rows - cols) <= SMOOTH_HALF, 1.0, 0.0).astype(BF16)
        r2 = lax.broadcasted_iota(jnp.int32, (256, 256), 0)
        c2 = lax.broadcasted_iota(jnp.int32, (256, 256), 1)
        eye[...] = jnp.where(r2 == c2, 1.0, 0.0).astype(BF16)
        f = lax.broadcasted_iota(jnp.int32, (BINS, 128), 0)
        count = jnp.minimum(f + SMOOTH_HALF, BINS - 1) - jnp.maximum(f - SMOOTH_HALF, 0) + 1
        invc[...] = 1.0 / count.astype(F32)

    nt = (((1,), (1,)), ((), ()))
    for v in range(STEP):
        re16, im16 = spec_ref[0, v], spec_ref[1, v]
        re, im = re16.astype(F32), im16.astype(F32)
        amp = jnp.sqrt(re * re + im * im).astype(BF16)
        amp2 = jnp.concatenate([amp, amp], axis=0)
        both = jnp.concatenate([re16, im16], axis=0)
        summed = lax.dot_general(band[...], amp2, nt, preferred_element_type=F32)
        flags = flags_ref[pl.ds(w * STEP + v, 1), :].astype(F32)
        flags = jnp.concatenate([flags, flags], axis=1)
        scale = flags / (summed * invc[...] + 1e-05)
        for h in range(2):
            half = lax.dot_general(
                eye[...], both[:, h * 256 : (h + 1) * 256], nt, preferred_element_type=F32
            )
            part = half * scale[h * 256 : (h + 1) * 256]
            white[v, h * 256 : (h + 1) * 256] = part.astype(BF16)
    for k in range(CHUNKS):
        for r in range(8):
            base = k * CBINS + ((z + r) & 7) * (2 * FC)
            for crel in range(2):
                start = pl.multiple_of(base + (c ^ crel) * FC, FC)
                for v in range(STEP):
                    outs[k * 8 + r][crel, w * STEP + v] = white[v, pl.ds(start, FC), :]
    core[0] = c


def whiten(spec, valid_flags, pos):
    shape = jax.ShapeDtypeStruct((2, WIN, FC, 128), BF16)
    full = pl.BlockSpec((2, WIN, FC, 128), lambda w, *_: (0, 0, 0, 0))
    return pl.pallas_call(
        whiten_kernel,
        out_shape=[shape] * (8 * CHUNKS) + [jax.ShapeDtypeStruct((1,), jnp.int32)],
        grid_spec=pltpu.PrefetchScalarGridSpec(
            num_scalar_prefetch=1,
            grid=(WIN // STEP,),
            in_specs=[
                pl.BlockSpec((2, STEP, CH, BINS), lambda w, *_: (0, w, 0, 0)),
                pl.BlockSpec((WIN, CH), lambda w, *_: (0, 0)),
            ],
            out_specs=[full] * (8 * CHUNKS) + [SM],
            scratch_shapes=[
                pltpu.VMEM((BINS, BINS), BF16),
                pltpu.VMEM((256, 256), BF16),
                pltpu.VMEM((BINS, 128), F32),
                pltpu.VMEM((STEP, BINS, 128), BF16),
            ],
        ),
        compiler_params=params(),
        cost_estimate=pl.CostEstimate(
            flops=3 * 512 * 512 * 128 * WIN, bytes_accessed=4 << 20, transcendentals=0
        ),
        name="whiten",
    )(pos, spec, valid_flags)


def merge_kernel(pos_ref, *refs):
    ins, (same, other) = refs[:8], refs[-2:]
    z = pos_ref[0]
    for n, r in enumerate(ORDER):
        src = (z - r) & 7
        same[src & 1, src >> 1] = ins[n][0]
        other[src & 1, src >> 1] = ins[n][1]


def merge(pieces, pos, *after):
    shape = jax.ShapeDtypeStruct((2, 4, WIN, FC, 128), BF16)
    return pl.pallas_call(
        merge_kernel,
        out_shape=[shape] * 2,
        in_specs=[SM] + [VM] * 8 + [ANY] * len(after),
        out_specs=[VM] * 2,
        compiler_params=params(),
        cost_estimate=pl.CostEstimate(
            flops=0, bytes_accessed=4 * 8 * WIN * FC * 256, transcendentals=0
        ),
        name="merge",
    )(pos, *pieces, *after)


def cross_kernel(pos_ref, own0, own1, prev0, prev1, *refs):
    outs, (wide, res) = refs[-10:-2], refs[-2:]
    z, c = pos_ref[0], pos_ref[1]
    rows = 4 * WIN * FC
    for n, (first, second) in enumerate(((own0, own1), (prev0, prev1))):
        for b in range(2):
            base = (n * 2 + b) * 2 * rows
            wide[base : base + rows] = first[b].reshape(rows, 128).astype(F32)
            wide[base + rows : base + 2 * rows] = second[b].reshape(rows, 128).astype(F32)
    sign = jnp.where(lax.broadcasted_iota(jnp.int32, (CH, 128), 1) < CH, 1.0, -1.0).astype(F32)
    tn = (((0,), (0,)), ((), ()))

    def one_bin(f, carry):
        x = [
            wide[pl.ds(n * 2 * rows + f, 8 * WIN, stride=FC), :].astype(BF16) for n in range(4)
        ]
        own_a, own_b, prev_a, prev_b = x
        for b, (left, rights) in enumerate(
            ((own_a, (prev_b, prev_a)), (own_b, (own_a, prev_b)))
        ):
            g = lax.dot_general(
                left, jnp.concatenate(rights, axis=1), tn, preferred_element_type=F32
            )
            for rnd in range(2):
                top = g[:CH, rnd * 128 : rnd * 128 + 128]
                bottom = pltpu.roll(g[CH:, rnd * 128 : rnd * 128 + 128], CH, 1)
                start = pl.multiple_of(((rnd * 2 + b) * FC + f) * CH, CH)
                res[pl.ds(start, CH), :] = bottom + sign * top
        return carry

    lax.fori_loop(0, FC, one_bin, 0, unroll=4)
    for r in range(8):
        dst = (z + r) & 7
        for crel in range(2):
            row = ((dst >> 1) * 2 + (c ^ crel)) * 8
            for rnd in range(2):
                base = (rnd * 2 + (dst & 1)) * FC * CH + row
                for i in range(8):
                    outs[r][crel, rnd, i] = res[pl.ds(base + i, FC, stride=CH), :].astype(BF16)


def cross(own0, own1, prev0, prev1, pos, *after):
    shape = jax.ShapeDtypeStruct((2, 2, 8, FC, 128), BF16)
    return pl.pallas_call(
        cross_kernel,
        out_shape=[shape] * 8,
        in_specs=[SM] + [VM] * 4 + [ANY] * len(after),
        out_specs=[VM] * 8,
        scratch_shapes=[
            pltpu.VMEM((32 * WIN * FC + FC, 128), F32),
            pltpu.VMEM((4 * FC * CH + CH, 128), F32),
        ],
        compiler_params=params(),
        cost_estimate=pl.CostEstimate(
            flops=4 * FC * 128 * 256 * 256, bytes_accessed=3 << 20, transcendentals=0
        ),
        name="cross",
    )(pos, own0, own1, prev0, prev1, *after)


def turn_kernel(order, pos_ref, *refs):
    ins, (out, buf) = refs[:8], refs[-2:]
    z = pos_ref[0]

    @pl.loop(0, 2)
    def _(rnd):
        for i in range(8):
            slot = i & 1
            for n, r in enumerate(order):
                start = pl.multiple_of(((z - r) & 7) * FC, FC)
                buf[slot, pl.ds(start, FC), :] = ins[n][0, rnd, i].astype(F32)
            out[rnd, i] = buf[slot].T.astype(BF16)


def turn(order, crel, pieces, pos, *after):
    half = pl.BlockSpec((1, 2, 8, FC, 128), lambda n: (crel, 0, 0, 0, 0))
    whole = pl.BlockSpec((2, 8, 128, 8 * FC), lambda n: (0, 0, 0, 0))
    return pl.pallas_call(
        functools.partial(turn_kernel, order),
        out_shape=jax.ShapeDtypeStruct((2, 8, 128, 8 * FC), BF16),
        grid=(1,),
        in_specs=[SM] + [half] * 8 + [ANY] * len(after),
        out_specs=whole,
        scratch_shapes=[pltpu.VMEM((2, 8 * FC, 128), F32)],
        compiler_params=params(),
        cost_estimate=pl.CostEstimate(flops=0, bytes_accessed=2 << 20, transcendentals=0),
        name="turn",
    )(pos, *pieces, *after)


def invert_kernel(scaling, chunk, *refs):
    parts, table, sums, out = refs[:2], refs[2], refs[3:-1], refs[-1]
    total = 0.0
    for k in range(2):
        rows = []
        for i in range(4):
            cols = [p[0, i, k * CH : (k + 1) * CH] for p in parts]
            rows.append(jnp.concatenate(cols, axis=1))
        total += jnp.dot(
            jnp.concatenate(rows, axis=0), table[k], preferred_element_type=F32
        )
    total = total.reshape(4, CH, LAG_COUNT)
    for ref in sums:
        total += ref[0]
    if chunk == CHUNKS - 1:
        total = total * scaling
    out[0] = total.astype(out.dtype)


def invert(chunk, parts, table, sums, scaling):
    part = pl.BlockSpec((1, 4, 128, 8 * FC), lambda r, i: (r, i, 0, 0))
    block = pl.BlockSpec((1, 4, CH, LAG_COUNT), lambda r, i: (r, i, 0, 0))
    dtype = BF16 if chunk == CHUNKS - 1 else F32
    return pl.pallas_call(
        functools.partial(invert_kernel, scaling, chunk),
        out_shape=jax.ShapeDtypeStruct((2, 8, CH, LAG_COUNT), dtype),
        grid=(2, 2),
        in_specs=[part] * 2
        + [pl.BlockSpec((2, CBINS, LAG_COUNT), lambda r, i: (0, chunk, 0))]
        + [block] * len(sums),
        out_specs=block,
        compiler_params=params(),
        cost_estimate=pl.CostEstimate(
            flops=1024 * 1024 * 1024, bytes_accessed=6 << 20, transcendentals=0
        ),
        name="invert",
    )(*parts, table.reshape(2, BINS, LAG_COUNT), *sums)


def turns(freq_ids, delay_ids):
    angles = jnp.mod(freq_ids * delay_ids, WIN_SAMPLES).astype(F32) * (2.0 * math.pi / WIN_SAMPLES)
    return jnp.cos(angles), jnp.sin(angles)


def lag_table(core):
    n = lax.broadcasted_iota(jnp.int32, (BINS, 1), 0)
    fine = n % FC
    z = (n // FC) % 8
    part = (n // (8 * FC)) % 2
    chunk = n // (16 * FC)
    freq_ids = chunk * CBINS + z * (2 * FC) + (part ^ core) * FC + fine + BAND_START
    lane = lax.broadcasted_iota(jnp.int32, (BINS, 128), 1)
    coarse = lane % 8 * 128 - LAG_COUNT // 2
    return *turns(freq_ids, lane), *turns(freq_ids, coarse)


def table_kernel(cos_a, sin_a, cos_b, sin_b, *refs):
    out = refs[-1]
    ca, sa, cb, sb = cos_a[...], sin_a[...], cos_b[...], sin_b[...]
    for n in range(LAG_COUNT // 128):
        c, s = cb[:, n : n + 1], sb[:, n : n + 1]
        out[:BINS, n * 128 : n * 128 + 128] = (ca * c - sa * s).astype(BF16)
        out[BINS:, n * 128 : n * 128 + 128] = (-(sa * c + ca * s)).astype(BF16)


def join_table(parts):
    return pl.pallas_call(
        table_kernel,
        out_shape=jax.ShapeDtypeStruct((2 * BINS, LAG_COUNT), BF16),
        in_specs=[VM] * 4,
        out_specs=VM,
        compiler_params=params(),
        cost_estimate=pl.CostEstimate(flops=8 << 20, bytes_accessed=4 << 20, transcendentals=0),
        name="table",
    )(*parts)


def place(z):
    return (z % 2) * 4 + z // 2


def device(m, z, c):
    return (m % 16) * 16 + place(z % 8) * 2 + c


EVERY = [(m, z, c) for m in range(16) for z in range(8) for c in range(2)]


def send(value, target):
    return lax.ppermute(value, ALL, [(device(*d), device(*target(*d))) for d in EVERY])


def round_ring(pieces, order=ORDER):
    got = []
    for r in order:
        got.append(send(pieces[r], lambda m, z, c: (m, z + r, c)) if r else pieces[r])
    return got


def other_core(value):
    return send(value, lambda m, z, c: (m, z, 1 - c))


def shards(spectra, valid_flags):
    z = 2 * lax.axis_index("zh") + lax.axis_index("zl")
    pos = jnp.stack([z, lax.axis_index("c")]).astype(jnp.int32)
    windows = spectra.shape[0] * lax.axis_size(("zh", "c"))
    scaling = 1.0 / math.sqrt(windows * BINS)
    *white, core = whiten(jnp.transpose(spectra, (2, 0, 1, 3)), valid_flags, pos)
    table = join_table(lag_table(core[0]))
    sums = ()
    merged, crossed = (), ()
    for k in range(CHUNKS):
        got = round_ring(white[k * 8 : k * 8 + 8])
        same, other = merge(got, pos, *merged)
        merged = (same, table)
        prev0 = send(same, lambda m, z, c: (m + 1, z, c))
        prev1 = send(other, lambda m, z, c: (m + 1, z, 1 - c))
        own1 = other_core(other)
        out = cross(same, own1, prev0, prev1, pos, *crossed)
        crossed = (out[0],)
        order = ORDER if k == 0 else FAR
        got = round_ring(out, order)
        other = turn(order, 1, got, pos, *sums)
        received = other_core(other)
        same = turn(order, 0, got, pos, other)
        sums = (invert(k, [same, received], table, sums, scaling),)
    return sums[0]


def solution(mesh):
    grid = mesh.devices.reshape(4, 4, 2, 4, 2)
    fine = Mesh(grid, ("x", "y", "zl", "zh", "c"))
    blk, seg = ("x", "y", "zl"), ("zh", "c")
    in_specs = (P(seg, blk, None, None), P(seg, blk))
    out_specs = P(None, blk + seg, None, None)


    return jax.shard_map(shards, mesh=fine, in_specs=in_specs, out_specs=out_specs, check_vma=False)
```
